32 devices in a mesh: dp: 8 (over z, x), seq: 4 (over y, core).
Axes of the slice: x: 2, y: 2, z: 4, core: 2. Of those that a mesh axis runs over, the one named last changes fastest.
Arguments:
- inputs: bfloat16 [8, 2048, 768], P('dp', 'seq'), may hold values from -2.5 to 2.5
- cotangent: bfloat16 [8, 2048, 768], P('dp', 'seq'), may hold values from -6 to 6
- qkv_weight: float32 [768, 2304], P('seq', 'dp'), may hold values from -0.21875 to 0.21875
- qkv_first: float32 [768, 2304], P('seq', 'dp'), may hold values from -128 to 128
- qkv_second: float32 [768, 2304], P('seq', 'dp'), may hold values from 491.52 to 4096
- out_weight: float32 [768, 768], P('seq', 'dp'), may hold values from -2.5 to 2.5
- out_first: float32 [768, 768], P('seq', 'dp'), may hold values from -13.57645 to 13.57645
- out_second: float32 [768, 768], P('seq', 'dp'), may hold values from 5.76 to 46.08
- fc_weight: float32 [768, 3072], P('seq', 'dp'), may hold values from -0.21875 to 0.21875
- fc_first: float32 [768, 3072], P('seq', 'dp'), may hold values from -46.08 to 46.08
- fc_second: float32 [768, 3072], P('seq', 'dp'), may hold values from 65.536 to 524.288
- proj_weight: float32 [3072, 768], P('seq', 'dp'), may hold values from -0.109375 to 0.109375
- proj_first: float32 [3072, 768], P('seq', 'dp'), may hold values from -97.28 to 97.28
- proj_second: float32 [3072, 768], P('seq', 'dp'), may hold values from 294.912 to 2359.296
- vectors: float32 [12, 768], P('seq', 'dp'), may hold values from -0.4 to 1.4, as said below
- vector_first: float32 [12, 768], P('seq', 'dp'), may hold values from -128 to 128
- vector_second: float32 [12, 768], P('seq', 'dp'), may hold values from 327.68 to 4096
Outputs:
- outputs: bfloat16 [8, 2048, 768], P('dp', 'seq')
- input_grad: bfloat16 [8, 2048, 768], P('dp', 'seq')
- qkv_first_new: float32 [768, 2304], P('seq', 'dp')
- qkv_second_new: float32 [768, 2304], P('seq', 'dp')
- qkv_updated: float32 [768, 2304], P('seq', 'dp')
- qkv_lowered: bfloat16 [768, 2304], P('seq', 'dp')
- out_first_new: float32 [768, 768], P('seq', 'dp')
- out_second_new: float32 [768, 768], P('seq', 'dp')
- out_updated: float32 [768, 768], P('seq', 'dp')
- out_lowered: bfloat16 [768, 768], P('seq', 'dp')
- fc_first_new: float32 [768, 3072], P('seq', 'dp')
- fc_second_new: float32 [768, 3072], P('seq', 'dp')
- fc_updated: float32 [768, 3072], P('seq', 'dp')
- fc_lowered: bfloat16 [768, 3072], P('seq', 'dp')
- proj_first_new: float32 [3072, 768], P('seq', 'dp')
- proj_second_new: float32 [3072, 768], P('seq', 'dp')
- proj_updated: float32 [3072, 768], P('seq', 'dp')
- proj_lowered: bfloat16 [3072, 768], P('seq', 'dp')
- vector_first_new: float32 [12, 768], P('seq', 'dp')
- vector_second_new: float32 [12, 768], P('seq', 'dp')
- vector_updated: float32 [12, 768], P('seq', 'dp')
- vector_lowered: bfloat16 [12, 768], P('seq', 'dp')
The draws below stay inside these ranges and needn't reach their ends.
Inputs may be any that keep to these rules, and one draw needn't show every extreme that they name: `vectors`: rows 0 and 5 are LayerNorm gains near one, the other rows are biases of order a tenth.
All inputs are finite; a program needn't handle non-finite values.
Results may differ from the reference program's by a relative error of at most 0.018.
Values may be sent and summed in bfloat16 or wider, within the bound.
No kernel may reach another device: no remote copies, remote signals or barrier semaphores. Data moves between devices by JAX's collectives and lax.ppermute only.
A program may use at most 192 MiB of HBM per device.

```python
import math
import jax
import jax.numpy as jnp
from jax import lax

D = 768
HEADS = 12
HEAD_DIM = 64
FF = 3072
DEPTH = 12
LEN = 2048
STEP = 10
SEQS = 8
TOKENS = 16384
NVEC = 12


def draw_vectors(key, part):
    noise = jnp.clip(jax.random.normal(key, (NVEC, D), jnp.float32), -4.0, 4.0)
    row_index = jnp.arange(NVEC)[:, None]
    gain_rows = (row_index == 0) | (row_index == 5)
    return jnp.where(gain_rows, 1.0 + 0.1 * noise, 0.1 * noise)


def steps_of(stream_key, dims, cuts, least, high):
    level, own = 1.0, jax.random.fold_in(stream_key, 6)
    for axis_at, blocks in cuts:
        heights = jnp.exp(jax.random.uniform(jax.random.fold_in(own, axis_at), (blocks,), jnp.float32, least / len(cuts), high / len(cuts)))
        level = level * jnp.repeat(heights, dims[axis_at] // blocks).reshape([-1 if axis == axis_at else 1 for axis in range(len(dims))])
    return level


def gaussian(key, shape, width, reach, shards=(), kind=jnp.bfloat16):
    loudness = steps_of(key, shape, shards, -0.22, 0.18) if shards else 1.0
    entries = jax.random.normal(key, shape, jnp.float32) * width * loudness
    return jnp.minimum(jnp.maximum(entries, -reach), reach).astype(kind)


def setup_inputs(seed: int = 0) -> dict:
    streams_of = jax.random.split(jax.random.key(seed), 18)
    inputs = gaussian(streams_of[0], (SEQS, LEN, D), 0.3, 2.5, ((0, 8), (1, 4)))
    cotangent = gaussian(streams_of[1], (SEQS, LEN, D), 1.0, 6.0, ((0, 8), (1, 4)))
    qkv_weight = gaussian(streams_of[2], (D, 3 * D), D ** -0.5, 0.21875, ((0, 4), (1, 8)), jnp.float32)
    qkv_first = gaussian(streams_of[3], (D, 3 * D), (0.25 * TOKENS ** 0.5), 128.0, ((0, 4), (1, 8)), jnp.float32)
    qkv_second = jnp.clip(jnp.exp(math.log(4096.0) - 2.1202636 * jax.random.uniform(streams_of[4], (D, 3 * D), jnp.float32) ** steps_of(streams_of[4], (D, 3 * D), ((0, 4), (1, 8)), -0.2, 0.2)), 491.52, 4096.0)
    out_weight = gaussian(streams_of[5], (D, D), (max(1, 16 * D // LEN)) ** -0.5, 2.5, ((0, 4), (1, 8)), jnp.float32)
    out_first = gaussian(streams_of[6], (D, D), (0.3 * (16 * SEQS) ** 0.5), 13.57645, ((0, 4), (1, 8)), jnp.float32)
    out_second = jnp.clip(jnp.exp(math.log(46.08) - 2.0794415 * jax.random.uniform(streams_of[7], (D, D), jnp.float32) ** steps_of(streams_of[7], (D, D), ((0, 4), (1, 8)), -0.2, 0.2)), 5.76, 46.08)
    fc_weight = gaussian(streams_of[8], (D, FF), D ** -0.5, 0.21875, ((0, 4), (1, 8)), jnp.float32)
    fc_first = gaussian(streams_of[9], (D, FF), (0.09 * TOKENS ** 0.5), 46.08, ((0, 4), (1, 8)), jnp.float32)
    fc_second = jnp.clip(jnp.exp(math.log(524.288) - 2.0794415 * jax.random.uniform(streams_of[10], (D, FF), jnp.float32) ** steps_of(streams_of[10], (D, FF), ((0, 4), (1, 8)), -0.2, 0.2)), 65.536, 524.288)
    proj_weight = gaussian(streams_of[11], (FF, D), FF ** -0.5, 0.109375, ((0, 4), (1, 8)), jnp.float32)
    proj_first = gaussian(streams_of[12], (FF, D), (0.19 * TOKENS ** 0.5), 97.28, ((0, 4), (1, 8)), jnp.float32)
    proj_second = jnp.clip(jnp.exp(math.log(2359.296) - 2.0794415 * jax.random.uniform(streams_of[13], (FF, D), jnp.float32) ** steps_of(streams_of[13], (FF, D), ((0, 4), (1, 8)), -0.2, 0.2)), 294.912, 2359.296)
    vectors = draw_vectors(jax.random.fold_in(streams_of[17], 71), 0)
    vector_first = gaussian(streams_of[15], (NVEC, D), (0.25 * TOKENS ** 0.5), 128.0, ((0, 4), (1, 8)), jnp.float32)
    vector_second = jnp.clip(jnp.exp(math.log(4096.0) - 2.5257287 * jax.random.uniform(streams_of[16], (NVEC, D), jnp.float32) ** steps_of(streams_of[16], (NVEC, D), ((0, 4), (1, 8)), -0.2, 0.2)), 327.68, 4096.0)
    return {"inputs": inputs, "cotangent": cotangent, "qkv_weight": qkv_weight, "qkv_first": qkv_first, "qkv_second": qkv_second, "out_weight": out_weight, "out_first": out_first, "out_second": out_second, "fc_weight": fc_weight, "fc_first": fc_first, "fc_second": fc_second, "proj_weight": proj_weight, "proj_first": proj_first, "proj_second": proj_second, "vectors": vectors, "vector_first": vector_first, "vector_second": vector_second}


@jax.custom_vjp
def low(v):
    return lax.optimization_barrier(v.astype(jnp.bfloat16)).astype(jnp.float32)

@jax.custom_vjp
def low_back(v):
    return v

def low_keep(v):
    return (low(v), None)

def low_pass(kept, grad):
    return (grad,)

def back_keep(v):
    return (v, None)

def back_low(kept, grad):
    return (low(grad),)
low.defvjp(low_keep, low_pass)
low_back.defvjp(back_keep, back_low)
beta_one = 0.5
beta_two = 0.5
highest = lax.Precision.HIGHEST

def rounded(values):
    return lax.optimization_barrier(values.astype(jnp.bfloat16)).astype(jnp.float32)

def layer_norm(values, gain, shift):
    centre = values - lax.optimization_barrier(jnp.mean(values, -1, keepdims=True))
    spread = lax.optimization_barrier(jnp.mean(centre * centre, -1, keepdims=True))
    return centre * lax.rsqrt(spread + 1e-05) * gain + shift

def attention(query, keys, values):
    block_len = min(512, LEN)
    block_count = LEN // block_len
    score_scale = HEAD_DIM ** (-0.5)
    blocks = query.reshape(HEADS, block_count, block_len, HEAD_DIM).transpose(1, 0, 2, 3)
    starts = (jnp.arange(block_count, dtype=jnp.int32) * block_len).astype(jnp.int32)

    @jax.checkpoint
    def one_block(pair):
        query_blk, block_start = pair
        scores = jnp.einsum('hqd,hkd->hqk', query_blk, keys, precision=highest) * score_scale
        scores = low_back(scores)
        query_pos = block_start + jnp.arange(block_len, dtype=jnp.int32)[None, :, None]
        key_pos = jnp.arange(LEN, dtype=jnp.int32)[None, None, :]
        scores = jnp.where(key_pos <= query_pos, scores, -1e+30)
        row_max = lax.optimization_barrier(jnp.max(scores, -1, keepdims=True))
        exponent = jnp.exp(scores - row_max)
        attn_probs = low(exponent / lax.optimization_barrier(jnp.sum(exponent, -1, keepdims=True)))
        return jnp.einsum('hqk,hkd->hqd', attn_probs, values, precision=highest)
    result = lax.map(one_block, (blocks, starts))
    return result.transpose(1, 0, 2, 3).reshape(HEADS, LEN, HEAD_DIM)

def adam_update(master, first, second, grad, rate, decay):
    first_new = beta_one * first + (1.0 - beta_one) * grad
    second_new = beta_two * second + (1.0 - beta_two) * grad * grad
    fix_one = 1.0 - beta_one ** STEP
    fix_two = 1.0 - beta_two ** STEP
    direction = first_new / fix_one / (jnp.sqrt(second_new / fix_two) + 1e-08)
    updated = master - rate * (direction + decay * master)
    return (first_new, second_new, updated, updated.astype(jnp.bfloat16))

def reference(inputs, cotangent, qkv_weight, qkv_first, qkv_second, out_weight, out_first, out_second, fc_weight, fc_first, fc_second, proj_weight, proj_first, proj_second, vectors, vector_first, vector_second):
    branch = DEPTH ** (-0.5)
    used = (rounded(qkv_weight), rounded(out_weight), rounded(fc_weight), rounded(proj_weight), rounded(vectors))

    def forward(tokens_in, w_qkv, w_out, w_fc, w_proj, vecs):
        h_one = low(layer_norm(tokens_in, vecs[0], vecs[1]))
        qkv_bias = jnp.concatenate([vecs[2], jnp.zeros_like(vecs[2]), vecs[3]])
        qkv_rows = low(low_back(jnp.dot(h_one, w_qkv, precision=highest) + qkv_bias))
        heads_all = qkv_rows.reshape(LEN, 3, HEADS, HEAD_DIM).transpose(1, 2, 0, 3)
        attn_heads = attention(heads_all[0], heads_all[1], heads_all[2])
        attn_rows = low(low_back(attn_heads.transpose(1, 0, 2).reshape(LEN, D)))
        attn_out = low_back(jnp.dot(attn_rows, w_out, precision=highest) + vecs[4])
        middle = tokens_in + branch * attn_out
        h_two = low(layer_norm(middle, vecs[5], vecs[6]))
        hidden = low_back(jnp.dot(h_two, w_fc, precision=highest) + vecs[8:].reshape(FF))
        active = low(jax.nn.gelu(hidden, approximate=True))
        mlp_out = low_back(jnp.dot(active, w_proj, precision=highest) + vecs[7])
        return middle + branch * mlp_out

    def one_seq(totals, pair):
        seq_in, seq_grad = pair
        result, pull = jax.vjp(forward, seq_in.astype(jnp.float32), used[0], used[1], used[2], used[3], used[4])
        grads = pull(seq_grad.astype(jnp.float32))
        totals = tuple((total + grad for total, grad in zip(totals, grads[1:])))
        return (totals, (result.astype(jnp.bfloat16), grads[0].astype(jnp.bfloat16)))
    zeros = tuple((jnp.zeros_like(weight) for weight in used))
    totals, (outputs, input_grad) = lax.scan(one_seq, zeros, (inputs, cotangent))
    rates = (D ** (-0.5), max(1, 16 * D // LEN) ** (-0.5), D ** (-0.5), FF ** (-0.5), 0.5)
    qkv_new = adam_update(qkv_weight, qkv_first, qkv_second, totals[0], rates[0], 0.1)
    out_new = adam_update(out_weight, out_first, out_second, totals[1], rates[1], 0.1)
    fc_new = adam_update(fc_weight, fc_first, fc_second, totals[2], rates[2], 0.1)
    proj_new = adam_update(proj_weight, proj_first, proj_second, totals[3], rates[3], 0.1)
    vec_new = adam_update(vectors, vector_first, vector_second, totals[4], rates[4], 0.0)
    return (outputs, input_grad, qkv_new[0], qkv_new[1], qkv_new[2], qkv_new[3], out_new[0], out_new[1], out_new[2], out_new[3], fc_new[0], fc_new[1], fc_new[2], fc_new[3], proj_new[0], proj_new[1], proj_new[2], proj_new[3], vec_new[0], vec_new[1], vec_new[2], vec_new[3])
```

```python
import functools

import jax
import jax.numpy as jnp
from jax import lax
from jax.experimental import pallas as pl
from jax.experimental.pallas import tpu as pltpu
from jax.sharding import PartitionSpec as P

D = 768
HEADS = 12
HEAD_DIM = 64
FF = 3072
DEPTH = 12
LEN = 2048
STEP = 10
PARTS = 4
TOK = LEN // PARTS
OWN_HEADS = HEADS // PARTS
GROUP = OWN_HEADS * HEAD_DIM
ROWS = D // PARTS
FB = 8
FC = FF // FB
DB = D // FB
QB = 3 * D // FB
BRANCH = DEPTH ** (-0.5)
EPS = 1e-05

beta_one = 0.5
beta_two = 0.5
matrix_decay = 0.1

f32 = jnp.float32
bf16 = jnp.bfloat16

NN = (((1,), (0,)), ((), ()))
NT = (((1,), (1,)), ((), ()))
TN = (((0,), (0,)), ((), ()))


def dg(left, right, dims):
    return lax.dot_general(left, right, dims, preferred_element_type=f32)


def adam_update(master, first, second, grad, rate, decay):
    first_new = beta_one * first + (1.0 - beta_one) * grad
    second_new = beta_two * second + (1.0 - beta_two) * grad * grad
    fix_one = 1.0 - beta_one**STEP
    fix_two = 1.0 - beta_two**STEP
    direction = first_new / fix_one / (jnp.sqrt(second_new / fix_two) + 1e-08)
    updated = master - rate * (direction + decay * master)
    return (first_new, second_new, updated, updated.astype(bf16))


def swap(value, axis, k):
    n = lax.axis_size(axis)
    return lax.ppermute(value, axis, [(i, i ^ k) for i in range(n)])


def tree_swap(values, axis, k):
    return [swap(v, axis, k) for v in values]


def gather_dp(block):
    z = [block] + [swap(block, "dp", 2 * k) for k in (1, 2, 3)]
    z = jnp.stack(z)
    other = swap(z, "dp", 1)
    return jnp.stack([z, other], 1).reshape((8,) + block.shape)


def add_low(left, right):
    return (left.astype(f32) + right.astype(f32)).astype(bf16)


VM = pl.BlockSpec(memory_space=pltpu.VMEM)
SM = pl.BlockSpec(memory_space=pltpu.SMEM)


def vmem_call(kernel, args, outs, scratch, flops, name):
    moved = sum(a.size * a.dtype.itemsize for a in args)
    moved += sum(o.size * o.dtype.itemsize for o in outs)
    return pl.pallas_call(
        kernel,
        out_shape=tuple(outs),
        in_specs=[SM] + [VM] * (len(args) - 1),
        out_specs=tuple([VM] * len(outs)),
        scratch_shapes=list(scratch),
        compiler_params=pltpu.CompilerParams(vmem_limit_bytes=60 * 2**20),
        cost_estimate=pl.CostEstimate(flops=flops, bytes_accessed=moved, transcendentals=0),
        name=name,
    )(*args)


def shape(dims, dtype):
    return jax.ShapeDtypeStruct(dims, dtype)


def norm_parts(values):
    centre = values - jnp.mean(values, -1, keepdims=True)
    spread = jnp.mean(centre * centre, -1, keepdims=True)
    scale = lax.rsqrt(spread + EPS)
    return centre * scale, scale


def pick_kernel(place, wq, o0, o1, o2, o3, whole):
    b, s = place[0], place[1]
    for k in range(FB):
        whole[pl.ds(pl.multiple_of((b ^ k) * QB, 16), QB), :] = wq[k]
    for k, out in enumerate((o0, o1, o2, o3)):
        for p in range(3):
            at = pl.multiple_of(p * D + (s ^ k) * GROUP, 16)
            out[p * GROUP : (p + 1) * GROUP, :] = whole[pl.ds(at, GROUP), :]


def forward_kernel(
    place, x0, x1, x2, x3, w0, w1, w2, w3, vec, qbias, vbias,
    qkv, wt, at0, at1, at2, at3, lse, pieces, heads_out,
):
    s = place[1]
    for k, w in enumerate((w0, w1, w2, w3)):
        pieces[s ^ k] = w[...]
    for m in range(PARTS):
        wt[:, m * ROWS : (m + 1) * ROWS] = pieces[m]
    bias = jnp.concatenate([qbias[s], jnp.zeros((1, GROUP), f32), vbias[s]], 1)
    for k, x in enumerate((x0, x1, x2, x3)):
        rows = pl.ds(pl.multiple_of((s ^ k) * TOK, TOK), TOK)
        hat, _ = norm_parts(x[...].astype(f32))
        h = (hat * vec[0:1, :] + vec[1:2, :]).astype(bf16)
        r = (dg(h, wt[...], NT) + bias).astype(bf16)
        for i in range(3 * OWN_HEADS):
            part = r[:, i * HEAD_DIM : (i + 1) * HEAD_DIM]
            if i < OWN_HEADS:
                part = (part.astype(f32) * HEAD_DIM ** (-0.5)).astype(bf16)
            qkv[i, rows, :] = part

    def head(h, _):
        for i in range(PARTS):
            qi = qkv[h, i * TOK : (i + 1) * TOK, :]
            n = (i + 1) * TOK
            sc = dg(qkv[OWN_HEADS + h, 0:n, :], qi, NT)
            kp = lax.broadcasted_iota(jnp.int32, (TOK, TOK), 0)
            qp = lax.broadcasted_iota(jnp.int32, (TOK, TOK), 1)
            last = jnp.where(kp <= qp, sc[i * TOK :], -1e30)
            mx = jnp.max(last, 0, keepdims=True)
            if i:
                mx = jnp.maximum(mx, jnp.max(sc[: i * TOK], 0, keepdims=True))
            e_last = jnp.exp(last - mx)
            total = jnp.sum(e_last, 0, keepdims=True)
            e = e_last.astype(bf16)
            if i:
                e_first = jnp.exp(sc[: i * TOK] - mx)
                total = total + jnp.sum(e_first, 0, keepdims=True)
                e = jnp.concatenate([e_first.astype(bf16), e], 0)
            o = dg(qkv[2 * OWN_HEADS + h, 0:n, :], e, TN) / total
            heads_out[h, i * TOK : (i + 1) * TOK, :] = o.T.astype(bf16)
            lse[h, :, i * TOK : (i + 1) * TOK] = mx + jnp.log(total)
        return 0

    lax.fori_loop(0, OWN_HEADS, head, 0)
    for k, at in enumerate((at0, at1, at2, at3)):
        rows = pl.ds(pl.multiple_of((s ^ k) * TOK, TOK), TOK)
        for h in range(OWN_HEADS):
            at[:, h * HEAD_DIM : (h + 1) * HEAD_DIM] = heads_out[h, rows, :]


def backward_kernel(
    place, qkv, g0, g1, g2, g3, at0, at1, at2, at3, lse, wt, x0, x1, x2, x3, vec,
    dh0, dh1, dh2, dh3, gq0, gq1, gq2, gq3, gnorm, gbias,
    gout, delta, dheads, dkt, dvt, gsum, gpieces,
):
    s = place[1]
    for k, (g, at) in enumerate(zip((g0, g1, g2, g3), (at0, at1, at2, at3))):
        rows = pl.ds(pl.multiple_of((s ^ k) * TOK, TOK), TOK)
        gv = g[...]
        prod = gv.astype(f32) * at[...].astype(f32)
        for h in range(OWN_HEADS):
            lanes = slice(h * HEAD_DIM, (h + 1) * HEAD_DIM)
            gout[h, rows, :] = gv[:, lanes]
            delta[h, rows, :] = jnp.sum(prod[:, lanes], 1, keepdims=True)

    def head(h, _):
        for i in range(PARTS):
            cut = slice(i * TOK, (i + 1) * TOK)
            qi = qkv[h, cut, :]
            gi = gout[h, cut, :]
            di = delta[h, cut, :]
            li = lse[h, :, cut].T
            dq = jnp.zeros((TOK, HEAD_DIM), f32)
            for j in range(i + 1):
                keys = slice(j * TOK, (j + 1) * TOK)
                kj = qkv[OWN_HEADS + h, keys, :]
                vj = qkv[2 * OWN_HEADS + h, keys, :]
                sc = dg(qi, kj, NT)
                if j == i:
                    qp = lax.broadcasted_iota(jnp.int32, (TOK, TOK), 0)
                    kp = lax.broadcasted_iota(jnp.int32, (TOK, TOK), 1)
                    sc = jnp.where(kp <= qp, sc, -1e30)
                p = jnp.exp(sc - li)
                dp = dg(gi, vj, NT)
                ds = (p * (dp - di)).astype(bf16)
                dq = dq + dg(ds, kj, NN)
                dv = dg(gi, p.astype(bf16), TN)
                dk = dg(qi, ds, TN)
                if j == i:
                    dkt[:, keys] = dk
                    dvt[:, keys] = dv
                else:
                    dkt[:, keys] += dk
                    dvt[:, keys] += dv
            dheads[h, cut, :] = (dq * HEAD_DIM ** (-0.5)).astype(bf16)
        for j in range(PARTS):
            keys = slice(j * TOK, (j + 1) * TOK)
            dheads[OWN_HEADS + h, keys, :] = dkt[:, keys].T.astype(bf16)
            dheads[2 * OWN_HEADS + h, keys, :] = dvt[:, keys].T.astype(bf16)
        return 0

    lax.fori_loop(0, OWN_HEADS, head, 0)
    gsum[...] = jnp.zeros_like(gsum)
    gnorm[...] = jnp.zeros_like(gnorm)
    sums = jnp.zeros((1, 3 * GROUP), f32)
    for k, (x, dh) in enumerate(zip((x0, x1, x2, x3), (dh0, dh1, dh2, dh3))):
        rows = pl.ds(pl.multiple_of((s ^ k) * TOK, TOK), TOK)
        dqkv = jnp.concatenate([dheads[i, rows, :] for i in range(3 * OWN_HEADS)], 1)
        hat, _ = norm_parts(x[...].astype(f32))
        h = (hat * vec[0:1, :] + vec[1:2, :]).astype(bf16)
        gsum[...] += dg(dqkv, h, TN)
        sums = sums + jnp.sum(dqkv.astype(f32), 0, keepdims=True)
        part = dg(dqkv, wt[...], NN)
        dh[...] = part.astype(bf16)
        gnorm[0:1, :] += jnp.sum(part * hat, 0, keepdims=True)
        gnorm[1:2, :] += jnp.sum(part, 0, keepdims=True)
    gbias[...] = jnp.zeros_like(gbias)
    gbias[s] = sums
    for m in range(PARTS):
        gpieces[m] = gsum[:, m * ROWS : (m + 1) * ROWS].astype(bf16)
    for k, out in enumerate((gq0, gq1, gq2, gq3)):
        out[...] = gpieces[s ^ k]


def middle_kernel(
    place, a0, a1, a2, a3, x, cot, c0, c1, c2, c3, f0, f1, f2, f3, p0, p1, p2, p3, vec, fbias,
    out, act, du, h2, dm, da, dx1, d0, d1, d2, d3, gvec, gfb,
    wo, wf, wp, mid, macc, dacc,
):
    b, s = place[0], place[1]
    for k, c in enumerate((c0, c1, c2, c3)):
        for m in range(FB):
            wo[k, pl.ds(pl.multiple_of((b ^ m) * DB, 16), DB), :] = c[m]
    proj = dg(a0[...], wo[0], NT)
    for k, a in ((1, a1), (2, a2), (3, a3)):
        proj = proj + dg(a[...], wo[k], NT)
    x1 = x[...].astype(f32) + BRANCH * (proj + vec[4:5, :])
    mid[...] = x1
    hat, _ = norm_parts(x1)
    h2[...] = (hat * vec[5:6, :] + vec[6:7, :]).astype(bf16)
    low = (BRANCH * cot[...].astype(f32)).astype(bf16)
    dm[...] = low
    gvec[3:4, :] = jnp.sum(low.astype(f32), 0, keepdims=True)
    macc[...] = jnp.zeros_like(macc)
    dacc[...] = jnp.zeros_like(dacc)

    def chunk(t, _):
        k = t // 2
        j = t % 2
        f = 2 * (s ^ k) + j
        for m, w in enumerate((f0, f1, f2, f3)):
            wf[pl.ds(pl.multiple_of((s ^ m) * ROWS, 16), ROWS), :] = w[f ^ b]
        for q, w in enumerate((p0, p1, p2, p3)):

            @pl.when(k == q)
            def _():
                for m in range(FB):
                    wp[pl.ds(pl.multiple_of((b ^ m) * DB, 16), DB), :] = w[
                        m, :, pl.ds(pl.multiple_of(j * FC, FC), FC)
                    ]

        u = dg(h2[...], wf[...], NN) + fbias[f]
        coef = (2.0 / jnp.pi) ** 0.5
        th = jnp.tanh(coef * (u + 0.044715 * (u * u * u)))
        half = 0.5 * (1.0 + th)
        av = (u * half).astype(bf16)
        act[f] = av
        slope = half + 0.5 * u * (1.0 - th * th) * (coef * (1.0 + 3 * 0.044715 * (u * u)))
        dv = (dg(dm[...], wp[...], NN) * slope).astype(bf16)
        du[f] = dv
        gfb[f] = jnp.sum(dv.astype(f32), 0, keepdims=True)
        macc[...] += dg(av, wp[...], NT)
        dacc[...] += dg(dv, wf[...], NT)
        return 0

    lax.fori_loop(0, FB, chunk, 0)
    x1 = mid[...]
    out[...] = (x1 + BRANCH * (macc[...] + vec[7:8, :])).astype(bf16)
    hat, scale = norm_parts(x1)
    dh = dacc[...]
    gvec[1:2, :] = jnp.sum(dh * hat, 0, keepdims=True)
    gvec[2:3, :] = jnp.sum(dh, 0, keepdims=True)
    e = dh * vec[5:6, :]
    back = scale * (e - jnp.mean(e, -1, keepdims=True) - hat * jnp.mean(e * hat, -1, keepdims=True))
    dx = cot[...].astype(f32) + back
    dx1[...] = dx
    dlow = (BRANCH * dx).astype(bf16)
    da[...] = dlow
    gvec[0:1, :] = jnp.sum(dlow.astype(f32), 0, keepdims=True)
    for k, o in enumerate((d0, d1, d2, d3)):
        o[...] = dg(dlow, wo[k], NN).astype(bf16)


def grads_kernel(
    place, act, du, h2, dm, da, a0, a1, a2, a3,
    gf_send, gf_keep, gp_send, gp_keep, go_send, go_keep, wide, narrow,
):
    b, s = place[0], place[1]

    def by_block(m, _):
        wide[...] = dg(h2[...], du[b ^ m], TN).astype(bf16)
        for k in range(PARTS):
            out = gf_send if k % 2 else gf_keep
            out[k // 2, m] = wide[pl.ds(pl.multiple_of((s ^ k) * ROWS, 16), ROWS), :]
        return 0

    lax.fori_loop(0, FB, by_block, 0)
    for k in range(PARTS):
        out = gp_send if k % 2 else gp_keep
        for j in range(2):
            wide[...] = dg(dm[...], act[2 * (s ^ k) + j], TN).astype(bf16)
            for m in range(FB):
                out[k // 2, m, :, j * FC : (j + 1) * FC] = wide[
                    pl.ds(pl.multiple_of((b ^ m) * DB, 16), DB), :
                ]
    for k, a in enumerate((a0, a1, a2, a3)):
        out = go_send if k % 2 else go_keep
        narrow[...] = dg(da[...], a[...], TN).astype(bf16)
        for m in range(FB):
            out[k // 2, m] = narrow[pl.ds(pl.multiple_of((b ^ m) * DB, 16), DB), :]


def arrange_kernel(place, g0, g1, g2, g3, out, whole):
    b, s = place[0], place[1]
    for k, g in enumerate((g0, g1, g2, g3)):
        for p in range(3):
            at = pl.multiple_of(p * D + (s ^ k) * GROUP, 16)
            whole[pl.ds(at, GROUP), :] = g[p * GROUP : (p + 1) * GROUP, :]
    for m in range(FB):
        out[m] = whole[pl.ds(pl.multiple_of((b ^ m) * QB, 16), QB), :]


def last_kernel(place, dx1, own, other, x, vec, out):
    hat, scale = norm_parts(x[...].astype(f32))
    e = (own[...].astype(f32) + other[...].astype(f32)) * vec[0:1, :]
    back = scale * (e - jnp.mean(e, -1, keepdims=True) - hat * jnp.mean(e * hat, -1, keepdims=True))
    out[...] = (dx1[...] + back).astype(bf16)


def local(
    inputs, cotangent,
    qkv_weight, qkv_first, qkv_second,
    out_weight, out_first, out_second,
    fc_weight, fc_first, fc_second,
    proj_weight, proj_first, proj_second,
    vectors, vector_first, vector_second,
):
    dp = lax.axis_size("dp")
    by_pairs = dp == FB
    b = lax.axis_index("dp").astype(jnp.int32)
    s = lax.axis_index("seq").astype(jnp.int32)
    place = jnp.stack([b if by_pairs else jnp.zeros_like(b), s])
    split = dp // FB

    x = [inputs.reshape(TOK, D)]
    cot = cotangent.reshape(TOK, D)
    x.append(swap(x[0], "seq", 1))
    x.append(swap(x[0], "seq", 2))
    x.append(swap(x[2], "seq", 1))

    low_qkv = qkv_weight.astype(bf16).T
    low_fc = fc_weight.astype(bf16)
    low_proj = proj_weight.astype(bf16).T
    low_out = out_weight.astype(bf16).T
    if by_pairs:
        all_qkv = gather_dp(low_qkv)
        all_fc = gather_dp(low_fc)
        all_proj = gather_dp(low_proj)
        all_out = gather_dp(low_out)
    else:
        all_qkv = lax.all_gather(low_qkv, "dp").reshape(FB, QB, ROWS)
        all_fc = lax.all_gather(low_fc, "dp").reshape(FB, split, ROWS, FC // split)
        all_fc = all_fc.transpose(0, 2, 1, 3).reshape(FB, ROWS, FC)
        all_proj = lax.all_gather(low_proj, "dp").reshape(FB, DB, D)
        all_out = lax.all_gather(low_out, "dp").reshape(FB, DB, ROWS)
    vec_blocks = lax.all_gather(vectors.astype(bf16), ("dp", "seq"))
    vec = vec_blocks.reshape(dp, PARTS, 3, D // dp).transpose(1, 2, 0, 3).reshape(12, D).astype(f32)
    qbias = vec[2].reshape(PARTS, 1, GROUP)
    vbias = vec[3].reshape(PARTS, 1, GROUP)
    fbias = vec[8:].reshape(FB, 1, FC)

    picked = vmem_call(
        pick_kernel, [place, all_qkv], [shape((3 * GROUP, ROWS), bf16)] * PARTS,
        [pltpu.VMEM((3 * D, ROWS), bf16)], 0, "pick",
    )
    wq = [picked[0]] + [swap(picked[k], "seq", k) for k in (1, 2, 3)]

    def others(value):
        second = swap(value, "seq", 2)
        return [value, swap(value, "seq", 1), second, swap(second, "seq", 1)]

    wo = others(all_out)
    wf = others(all_fc)
    wp = others(all_proj)

    qkv, wt, at0, at1, at2, at3, lse = vmem_call(
        forward_kernel, [place, *x, *wq, vec, qbias, vbias],
        [shape((3 * OWN_HEADS, LEN, HEAD_DIM), bf16), shape((3 * GROUP, D), bf16)]
        + [shape((TOK, GROUP), bf16)] * PARTS + [shape((OWN_HEADS, 1, LEN), f32)],
        [pltpu.VMEM((PARTS, 3 * GROUP, ROWS), bf16), pltpu.VMEM((OWN_HEADS, LEN, HEAD_DIM), bf16)],
        6 * 10**9, "forward",
    )
    at = [at0, at1, at2, at3]
    rows = [at[0]] + [swap(at[k], "seq", k) for k in (1, 2, 3)]

    (out, act, du, h2, dm, da, dx1, d0, d1, d2, d3, gvec, gfb) = vmem_call(
        middle_kernel, [place, *rows, x[0], cot, *wo, *wf, *wp, vec, fbias],
        [shape((TOK, D), bf16), shape((FB, TOK, FC), bf16), shape((FB, TOK, FC), bf16)]
        + [shape((TOK, D), bf16)] * 3 + [shape((TOK, D), f32)] + [shape((TOK, GROUP), bf16)] * PARTS
        + [shape((4, D), f32), shape((FB, 1, FC), f32)],
        [pltpu.VMEM((PARTS, D, GROUP), bf16), pltpu.VMEM((D, FC), bf16), pltpu.VMEM((D, FC), bf16),
         pltpu.VMEM((TOK, D), f32), pltpu.VMEM((TOK, D), f32), pltpu.VMEM((TOK, D), f32)],
        12 * 10**9, "middle",
    )
    gout = [d0] + [swap(d, "seq", k) for k, d in ((1, d1), (2, d2), (3, d3))]

    grads = vmem_call(
        grads_kernel, [place, act, du, h2, dm, da, *rows],
        [shape((2, FB, ROWS, FC), bf16)] * 2 + [shape((2, FB, DB, D), bf16)] * 2
        + [shape((2, FB, DB, ROWS), bf16)] * 2,
        [pltpu.VMEM((D, FC), bf16), pltpu.VMEM((D, GROUP), bf16)], 6 * 10**9, "grads",
    )

    def reduce_dp(value, first):
        pair = value.reshape((4, 2) + value.shape[1:])
        got = swap(pair[:, 1], "dp", 1)
        part = add_low(pair[:, 0], got)
        total = part[0].astype(f32)
        for k in (1, 2, 3):
            total = total + swap(part[k], "dp", 2 * k).astype(f32)
        return total

    def reduce_all(send, keep, order):
        got = swap(send, "seq", 1)
        if order == "yx":
            other = add_low(keep[1], got[1])
            mine = add_low(keep[0], got[0])
            mine = add_low(mine, swap(other, "seq", 2))
            return reduce_dp(mine, None)
        pair_k = keep.reshape((2, 4, 2) + keep.shape[2:])
        pair_g = got.reshape((2, 4, 2) + keep.shape[2:])
        other = add_low(pair_k[:, :, 1], pair_g[:, :, 1])
        mine = add_low(pair_k[:, :, 0], pair_g[:, :, 0])
        mine = add_low(mine, swap(other, "dp", 1))
        part = add_low(mine[0], swap(mine[1], "seq", 2))
        total = part[0].astype(f32)
        for k in (1, 2, 3):
            total = total + swap(part[k], "dp", 2 * k).astype(f32)
        return total

    def reduce_plain(send, keep, kind):
        got = swap(send, "seq", 1)
        mine = add_low(keep[0], got[0])
        mine = add_low(mine, swap(add_low(keep[1], got[1]), "seq", 2))
        return scatter_plain(mine, kind)

    def scatter_plain(mine, kind):
        if kind == "fc":
            mine = mine.reshape(FB, ROWS, split, FC // split).transpose(0, 2, 1, 3)
            mine = mine.reshape(dp, ROWS, FC // split)
        else:
            mine = mine.reshape((dp, -1) + mine.shape[2:])
        return lax.psum_scatter(mine, "dp", scatter_dimension=0, tiled=False).astype(f32)

    if by_pairs:
        sum_fc = reduce_all(grads[0], grads[1], "yx")
        sum_proj = reduce_all(grads[2], grads[3], "xy").T
        sum_out = reduce_all(grads[4], grads[5], "yx").T
    else:
        sum_fc = reduce_plain(grads[0], grads[1], "fc")
        sum_proj = reduce_plain(grads[2], grads[3], "proj").T
        sum_out = reduce_plain(grads[4], grads[5], "out").T

    (dh0, dh1, dh2, dh3, gq0, gq1, gq2, gq3, gnorm, gbias) = vmem_call(
        backward_kernel, [place, qkv, *gout, *at, lse, wt, *x, vec],
        [shape((TOK, D), bf16)] * PARTS + [shape((3 * GROUP, ROWS), bf16)] * PARTS
        + [shape((2, D), f32), shape((PARTS, 1, 3 * GROUP), f32)],
        [pltpu.VMEM((OWN_HEADS, LEN, HEAD_DIM), bf16), pltpu.VMEM((OWN_HEADS, LEN, 1), f32),
         pltpu.VMEM((3 * OWN_HEADS, LEN, HEAD_DIM), bf16), pltpu.VMEM((HEAD_DIM, LEN), f32),
         pltpu.VMEM((HEAD_DIM, LEN), f32), pltpu.VMEM((3 * GROUP, D), f32),
         pltpu.VMEM((PARTS, 3 * GROUP, ROWS), bf16)],
        12 * 10**9, "backward",
    )
    gq = [gq0] + [swap(g, "seq", k) for k, g in ((1, gq1), (2, gq2), (3, gq3))]
    (blocks,) = vmem_call(
        arrange_kernel, [place, *gq], [shape((FB, QB, ROWS), bf16)],
        [pltpu.VMEM((3 * D, ROWS), bf16)], 0, "arrange",
    )
    sum_qkv = (reduce_dp(blocks, None) if by_pairs else scatter_plain(blocks, "qkv")).T

    own = add_low(dh0, swap(dh1, "seq", 1))
    other = swap(add_low(dh2, swap(dh3, "seq", 1)), "seq", 2)
    (input_grad,) = vmem_call(
        last_kernel, [place, dx1, own, other, x[0], vec], [shape((TOK, D), bf16)], [], 0, "last"
    )

    gb = gbias.reshape(PARTS, 3, GROUP)
    grad_vec = jnp.concatenate(
        [
            gnorm,
            gb[:, 0].reshape(1, D),
            gb[:, 2].reshape(1, D),
            gvec,
            gfb.reshape(4, D),
        ],
        0,
    )
    total_vec = lax.psum(grad_vec, ("dp", "seq"))
    width = D // dp
    sum_vec = lax.dynamic_slice(total_vec, (s * 3, b * width), (3, width))

    qkv_new = adam_update(qkv_weight, qkv_first, qkv_second, sum_qkv, D ** (-0.5), matrix_decay)
    out_new = adam_update(
        out_weight, out_first, out_second, sum_out, max(1, 16 * D // LEN) ** (-0.5), matrix_decay
    )
    fc_new = adam_update(fc_weight, fc_first, fc_second, sum_fc, D ** (-0.5), matrix_decay)
    proj_new = adam_update(
        proj_weight, proj_first, proj_second, sum_proj, FF ** (-0.5), matrix_decay
    )
    vec_new = adam_update(vectors, vector_first, vector_second, sum_vec, 0.5, 0.0)
    return (
        out.reshape(inputs.shape),
        input_grad.reshape(inputs.shape),
        *qkv_new,
        *out_new,
        *fc_new,
        *proj_new,
        *vec_new,
    )


def solution(mesh):
    rows = P("dp", "seq", None)
    block = P("seq", "dp")
    return jax.shard_map(
        local,
        mesh=mesh,
        in_specs=(rows, rows) + (block,) * 15,
        out_specs=(rows, rows) + (block,) * 20,
        check_vma=False,
    )
```

```python
import functools

import jax
import jax.numpy as jnp
from jax import lax
from jax.experimental import pallas as pl
from jax.experimental.pallas import tpu as pltpu
from jax.sharding import PartitionSpec as P

D = 768
HEADS = 12
HEAD_DIM = 64
FF = 3072
DEPTH = 12
LEN = 2048
STEP = 10
PARTS = 4
TOK = LEN // PARTS
OWN_HEADS = HEADS // PARTS
GROUP = OWN_HEADS * HEAD_DIM
ROWS = D // PARTS
FB = 8
FC = FF // FB
DB = D // FB
QB = 3 * D // FB
QH = QB // 2
QP = QH + 8
HALF = DB // 2
AR = ROWS + HALF
LR = AR + ROWS
BRANCH = DEPTH ** (-0.5)
EPS = 1e-05

beta_one = 0.5
beta_two = 0.5
matrix_decay = 0.1

f32 = jnp.float32
bf16 = jnp.bfloat16

NN = (((1,), (0,)), ((), ()))
NT = (((1,), (1,)), ((), ()))
TN = (((0,), (0,)), ((), ()))


def dg(left, right, dims):
    return lax.dot_general(left, right, dims, preferred_element_type=f32)


def adam_update(master, first, second, grad, rate, decay):
    first_new = beta_one * first + (1.0 - beta_one) * grad
    second_new = beta_two * second + (1.0 - beta_two) * grad * grad
    fix_one = 1.0 - beta_one**STEP
    fix_two = 1.0 - beta_two**STEP
    direction = first_new / fix_one / (jnp.sqrt(second_new / fix_two) + 1e-08)
    updated = master - rate * (direction + decay * master)
    return (first_new, second_new, updated, updated.astype(bf16))


def swap(value, axis, k):
    n = lax.axis_size(axis)
    return lax.ppermute(value, axis, [(i, i ^ k) for i in range(n)])


def direct(pieces):
    return [pieces[0]] + [swap(pieces[k], "dp", 2 * k) for k in (1, 2, 3)]


def seq_exchange(values):
    return [values[0]] + [swap(values[k], "seq", k) for k in range(1, PARTS)]


def tie(*values):
    return lax.optimization_barrier(values)


VM = pl.BlockSpec(memory_space=pltpu.VMEM)
SM = pl.BlockSpec(memory_space=pltpu.SMEM)


def space(item):
    dims = list(item.shape)
    dims[-1] = -(-dims[-1] // 128) * 128
    if len(dims) > 1:
        dims[-2] = -(-dims[-2] // 8) * 8
    size = jnp.dtype(item.dtype).itemsize
    for d in dims:
        size *= d
    return size


def vmem_call(kernel, args, outs, scratch, flops, name, spare=4, deps=()):
    n = len(args)

    def body(*refs):
        kernel(*refs[:n], *refs[n + len(deps) :])

    need = sum(space(a) for a in (*args[1:], *outs, *scratch)) + spare * 2**20
    return pl.pallas_call(
        body,
        out_shape=tuple(outs),
        in_specs=[SM] + [VM] * (n - 1) + [pl.BlockSpec(memory_space=pl.ANY)] * len(deps),
        out_specs=tuple([VM] * len(outs)),
        scratch_shapes=list(scratch),
        compiler_params=pltpu.CompilerParams(vmem_limit_bytes=need),
        cost_estimate=pl.CostEstimate(
            flops=int(flops * 0.5e9), bytes_accessed=1024, transcendentals=0
        ),
        name=name,
    )(*args, *deps)


def shape(dims, dtype):
    return jax.ShapeDtypeStruct(dims, dtype)


def norm_parts(values):
    centre = values - jnp.mean(values, -1, keepdims=True)
    spread = jnp.mean(centre * centre, -1, keepdims=True)
    scale = lax.rsqrt(spread + EPS)
    return centre * scale, scale


def stack_kernel(place, p0, p1, p2, p3, out):
    for k, p in enumerate((p0, p1, p2, p3)):
        out[k] = p[...]


def pick_kernel(place, z, x, o0, o1, o2, o3, whole):
    b, s = place[0], place[1]
    for m in range(FB):
        part = (z, x)[m % 2]
        for i in range(2):
            whole[pl.ds(pl.multiple_of((b ^ m) * QB + i * QH, 16), QH), :] = part[
                m // 2, 0:QH, i * ROWS : (i + 1) * ROWS
            ]
    tail = jnp.concatenate(
        [
            (z, x)[m % 2][m // 2, QH : QH + 1, i * ROWS : (i + 1) * ROWS]
            for m in range(FB)
            for i in range(2)
        ],
        0,
    )
    for k, out in enumerate((o0, o1, o2, o3)):
        for p in range(3):
            at = pl.multiple_of(p * D + (s ^ k) * GROUP, 16)
            out[p * GROUP : (p + 1) * GROUP, :] = whole[pl.ds(at, GROUP), :]
        out[3 * GROUP :, :] = tail


def fold_kernel(place, *refs):
    n = len(refs) // 3
    for keep, got, out in zip(refs[:n], refs[n : 2 * n], refs[2 * n :]):

        def step(j, _):
            out[j] = (keep[j].astype(f32) + got[j].astype(f32)).astype(bf16)
            return 0

        lax.fori_loop(0, keep.shape[0], step, 0)


def pieces_kernel(place, keep, got, *outs):
    for k, out in enumerate(outs):
        out[...] = (keep[k].astype(f32) + got[k].astype(f32)).astype(bf16)


def split_kernel(place, keep, got, mine, other):
    def step(j, _):
        for i, out in enumerate((mine, other)):
            out[j] = (keep[i, j].astype(f32) + got[i, j].astype(f32)).astype(bf16)
        return 0

    lax.fori_loop(0, keep.shape[1], step, 0)


def line_kernel(place, keep, got, *outs):
    for k, out in enumerate(outs):
        j = (place[0] // 2) ^ k
        out[...] = (keep[j].astype(f32) + got[j].astype(f32)).astype(bf16)


def four_kernel(place, p0, p1, p2, p3, mine, other):
    for i, out in enumerate((mine, other)):
        total = (p0[i].astype(f32) + p1[i].astype(f32)) + (p2[i].astype(f32) + p3[i].astype(f32))
        out[...] = total.astype(out.dtype)


def attend(qkv, lse, heads_out):
    for i in range(PARTS):
        qi = qkv[0, i * TOK : (i + 1) * TOK, :]
        n = (i + 1) * TOK
        sc = dg(qkv[1, 0:n, :], qi, NT)
        kp = lax.broadcasted_iota(jnp.int32, (TOK, TOK), 0)
        qp = lax.broadcasted_iota(jnp.int32, (TOK, TOK), 1)
        last = jnp.where(kp <= qp, sc[i * TOK :], -1e30)
        mx = jnp.max(last, 0, keepdims=True)
        if i:
            mx = jnp.maximum(mx, jnp.max(sc[: i * TOK], 0, keepdims=True))
        e_last = jnp.exp(last - mx)
        total = jnp.sum(e_last, 0, keepdims=True)
        e = e_last.astype(bf16)
        if i:
            e_first = jnp.exp(sc[: i * TOK] - mx)
            total = total + jnp.sum(e_first, 0, keepdims=True)
            e = jnp.concatenate([e_first.astype(bf16), e], 0)
        o = dg(qkv[2, 0:n, :], e, TN) / total
        heads_out[i * TOK : (i + 1) * TOK, :] = o.T.astype(bf16)
        lse[:, i * TOK : (i + 1) * TOK] = mx + jnp.log(total)


def first_kernel(
    place, x0, x1, x2, x3, w0, w1, w2, w3,
    qkv0, qkv1, qkv2, wt, heads_out, lse, vec, fbias, pieces, blocks,
):
    b, s = place[0], place[1]
    for k, w in enumerate((w0, w1, w2, w3)):
        pieces[s ^ k] = w[0 : 3 * GROUP, :]
        tail = w[3 * GROUP :, :].astype(f32)
        for m in range(FB):
            blocks[s ^ k, b ^ m, 0:1, :] = tail[2 * m : 2 * m + 1, 0:DB]
            blocks[s ^ k, b ^ m, 1:2, :] = tail[2 * m : 2 * m + 1, DB : 2 * DB]
            blocks[s ^ k, b ^ m, 2:3, :] = tail[2 * m + 1 : 2 * m + 2, 0:DB]
    for j in range(PARTS):
        wt[:, j * ROWS : (j + 1) * ROWS] = pieces[j]
    qbias = jnp.zeros((1, GROUP), f32)
    vbias = jnp.zeros((1, GROUP), f32)
    for r in range(12):
        row = jnp.concatenate([blocks[r // 3, m, r % 3 : r % 3 + 1, :] for m in range(FB)], 1)
        vec[r : r + 1, :] = row
        for m in range(PARTS):
            mine = row[:, m * GROUP : (m + 1) * GROUP]
            if r == 2:
                qbias = jnp.where(s == m, mine, qbias)
            if r == 3:
                vbias = jnp.where(s == m, mine, vbias)
        for m in range(2):
            if r >= 8:
                fbias[2 * (r - 8) + m] = row[:, m * FC : (m + 1) * FC]
    bias = jnp.concatenate([qbias, jnp.zeros((1, GROUP), f32), vbias], 1)
    for k, x in enumerate((x0, x1, x2, x3)):
        rows = pl.ds(pl.multiple_of((s ^ k) * TOK, TOK), TOK)
        hat, _ = norm_parts(x[...].astype(f32))
        h = (hat * vec[0:1, :] + vec[1:2, :]).astype(bf16)
        r = (dg(h, wt[...], NT) + bias).astype(bf16)
        for i in range(3 * OWN_HEADS):
            part = r[:, i * HEAD_DIM : (i + 1) * HEAD_DIM]
            if i < OWN_HEADS:
                part = (part.astype(f32) * HEAD_DIM ** (-0.5)).astype(bf16)
            (qkv0, qkv1, qkv2)[i % OWN_HEADS][i // OWN_HEADS, rows, :] = part
    attend(qkv0, lse, heads_out)


def second_kernel(place, qkv, heads_out, lse):
    attend(qkv, lse, heads_out)


def third_kernel(place, qkv, head0, head1, at0, at1, at2, at3, lse, head2):
    s = place[1]
    attend(qkv, lse, head2)
    for k, at in enumerate((at0, at1, at2, at3)):
        rows = pl.ds(pl.multiple_of((s ^ k) * TOK, TOK), TOK)
        for i, head in enumerate((head0, head1, head2)):
            at[:, i * HEAD_DIM : (i + 1) * HEAD_DIM] = head[rows, :]


def backward_kernel(
    place, qkv, g0, g1, g2, g3, at0, at1, at2, at3, lse,
    dheads, gout, delta, dkt, dvt, *, head,
):
    s = place[1]
    lanes = slice(head * HEAD_DIM, (head + 1) * HEAD_DIM)
    for k, (g, at) in enumerate(zip((g0, g1, g2, g3), (at0, at1, at2, at3))):
        rows = pl.ds(pl.multiple_of((s ^ k) * TOK, TOK), TOK)
        gv = g[:, lanes]
        gout[rows, :] = gv
        delta[rows, :] = jnp.sum(gv.astype(f32) * at[:, lanes].astype(f32), 1, keepdims=True)
    for i in range(PARTS):
        cut = slice(i * TOK, (i + 1) * TOK)
        qi = qkv[0, cut, :]
        gi = gout[cut, :]
        di = delta[cut, :]
        li = lse[:, cut].T
        dq = jnp.zeros((TOK, HEAD_DIM), f32)
        for j in range(i + 1):
            keys = slice(j * TOK, (j + 1) * TOK)
            kj = qkv[1, keys, :]
            vj = qkv[2, keys, :]
            sc = dg(qi, kj, NT)
            if j == i:
                qp = lax.broadcasted_iota(jnp.int32, (TOK, TOK), 0)
                kp = lax.broadcasted_iota(jnp.int32, (TOK, TOK), 1)
                sc = jnp.where(kp <= qp, sc, -1e30)
            p = jnp.exp(sc - li)
            dp = dg(gi, vj, NT)
            ds = (p * (dp - di)).astype(bf16)
            dq = dq + dg(ds, kj, NN)
            dv = dg(gi, p.astype(bf16), TN)
            dk = dg(qi, ds, TN)
            if j == i:
                dkt[:, keys] = dk
                dvt[:, keys] = dv
            else:
                dkt[:, keys] += dk
                dvt[:, keys] += dv
        dheads[0, cut, :] = (dq * HEAD_DIM ** (-0.5)).astype(bf16)
    for j in range(PARTS):
        keys = slice(j * TOK, (j + 1) * TOK)
        dheads[1, keys, :] = dkt[:, keys].T.astype(bf16)
        dheads[2, keys, :] = dvt[:, keys].T.astype(bf16)


def gather_kernel(
    place, e0, e1, e2, wt, x0, x1, x2, x3, vec, gvec, gfb,
    dk0, dk1, ds0, ds1, gq0, gq1, gq2, gq3, gsum, gpieces, gbias, rows_of,
):
    b, s = place[0], place[1]
    gsum[...] = jnp.zeros_like(gsum)
    sums = jnp.zeros((1, 3 * GROUP), f32)
    gain = jnp.zeros((1, D), f32)
    shift = jnp.zeros((1, D), f32)
    for k, x in enumerate((x0, x1, x2, x3)):
        rows = pl.ds(pl.multiple_of((s ^ k) * TOK, TOK), TOK)
        dqkv = jnp.concatenate([e[i, rows, :] for i in range(3) for e in (e0, e1, e2)], 1)
        hat, _ = norm_parts(x[...].astype(f32))
        h = (hat * vec[0:1, :] + vec[1:2, :]).astype(bf16)
        gsum[...] += dg(dqkv, h, TN)
        sums = sums + jnp.sum(dqkv.astype(f32), 0, keepdims=True)
        part = dg(dqkv, wt[...], NN)
        (dk0, ds0, dk1, ds1)[k][...] = part.astype(bf16)
        gain = gain + jnp.sum(part * hat, 0, keepdims=True)
        shift = shift + jnp.sum(part, 0, keepdims=True)
    for m in range(PARTS):
        gpieces[m] = gsum[:, m * ROWS : (m + 1) * ROWS].astype(bf16)
    for k, out in enumerate((gq0, gq1, gq2, gq3)):
        out[0 : 3 * GROUP, :] = gpieces[s ^ k]
    gbias[...] = jnp.zeros_like(gbias)
    gbias[s] = sums
    qrow = jnp.concatenate([gbias[m, :, 0:GROUP] for m in range(PARTS)], 1)
    vrow = jnp.concatenate([gbias[m, :, 2 * GROUP : 3 * GROUP] for m in range(PARTS)], 1)
    for r in range(12):
        if r < 4:
            row = (gain, shift, qrow, vrow)[r]
        elif r < 8:
            row = gvec[r - 4 : r - 3, :]
        else:
            row = jnp.concatenate([gfb[2 * (r - 8)], gfb[2 * (r - 8) + 1]], 1)
        for m in range(FB):
            rows_of[r // 3, m, r % 3 : r % 3 + 1, :] = row[:, m * DB : (m + 1) * DB]
    for k, out in enumerate((gq0, gq1, gq2, gq3)):
        tail = []
        for m in range(FB):
            part = rows_of[s ^ k, b ^ m]
            tail.append(jnp.concatenate([part[0:1, :], part[1:2, :]], 1))
            tail.append(jnp.concatenate([part[2:3, :], jnp.zeros((1, DB), f32)], 1))
        out[3 * GROUP :, :] = jnp.concatenate(tail, 0).astype(bf16)


def middle_kernel(
    place, a0, a1, a2, a3, x, cot, l0, l1, l2, l3, l4, l5, l6, l7,
    p0, p1, p2, p3, p4, p5, p6, p7, vec, fbias,
    out, act, du, h2, dm, da, dx1, d0, d1, d2, d3, gvec, gfb, wo, wf, wp, mid, macc, dacc,
):
    b, s = place[0], place[1]
    weights = (l0, l1, l2, l3, l4, l5, l6, l7)
    downs = (p0, p1, p2, p3, p4, p5, p6, p7)
    for k in range(PARTS):
        for m in range(FB):
            low = weights[4 * (k // 2) + 2 * (m % 2) + k % 2]
            for i in range(2):
                wo[k, pl.ds(pl.multiple_of((b ^ m) * DB + i * HALF, 16), HALF), :] = low[
                    (b // 2) ^ (m // 2), ROWS:AR, i * GROUP : (i + 1) * GROUP
                ]
    proj = dg(a0[...], wo[0], NT)
    for k, a in ((1, a1), (2, a2), (3, a3)):
        proj = proj + dg(a[...], wo[k], NT)
    x1 = x[...].astype(f32) + BRANCH * (proj + vec[4:5, :])
    mid[...] = x1
    hat, _ = norm_parts(x1)
    h2[...] = (hat * vec[5:6, :] + vec[6:7, :]).astype(bf16)
    low = (BRANCH * cot[...].astype(f32)).astype(bf16)
    dm[...] = low
    gvec[3:4, :] = jnp.sum(low.astype(f32), 0, keepdims=True)
    macc[...] = jnp.zeros_like(macc)
    dacc[...] = jnp.zeros_like(dacc)

    def chunk(z, _, q):
        j = (b % 2) ^ q
        f = 2 * z + j
        for m in range(PARTS):
            part = weights[4 * (m // 2) + 2 * q + m % 2]
            wf[pl.ds(pl.multiple_of((s ^ m) * ROWS, 16), ROWS), :] = part[z, 0:ROWS, :]
        for k in range(PARTS):

            @pl.when((s ^ z) == k)
            def _():
                for m in range(FB):
                    part = downs[4 * (k // 2) + 2 * (m % 2) + k % 2]
                    wp[pl.ds(pl.multiple_of((b ^ m) * DB, 16), DB), :] = part[
                        (b // 2) ^ (m // 2), pl.ds(pl.multiple_of(j * DB, 16), DB), :
                    ]

        u = dg(h2[...], wf[...], NN) + fbias[f]
        coef = (2.0 / jnp.pi) ** 0.5
        th = jnp.tanh(coef * (u + 0.044715 * (u * u * u)))
        half = 0.5 * (1.0 + th)
        av = (u * half).astype(bf16)
        act[f] = av
        slope = half + 0.5 * u * (1.0 - th * th) * (coef * (1.0 + 3 * 0.044715 * (u * u)))
        dv = (dg(dm[...], wp[...], NN) * slope).astype(bf16)
        du[f] = dv
        gfb[f] = jnp.sum(dv.astype(f32), 0, keepdims=True)
        macc[...] += dg(av, wp[...], NT)
        dacc[...] += dg(dv, wf[...], NT)
        return 0

    for q in range(2):
        lax.fori_loop(0, 4, functools.partial(chunk, q=q), 0)
    x1 = mid[...]
    out[...] = (x1 + BRANCH * (macc[...] + vec[7:8, :])).astype(bf16)
    hat, scale = norm_parts(x1)
    dh = dacc[...]
    gvec[1:2, :] = jnp.sum(dh * hat, 0, keepdims=True)
    gvec[2:3, :] = jnp.sum(dh, 0, keepdims=True)
    e = dh * vec[5:6, :]
    back = scale * (e - jnp.mean(e, -1, keepdims=True) - hat * jnp.mean(e * hat, -1, keepdims=True))
    dx = cot[...].astype(f32) + back
    dx1[...] = dx
    dlow = (BRANCH * dx).astype(bf16)
    da[...] = dlow
    gvec[0:1, :] = jnp.sum(dlow.astype(f32), 0, keepdims=True)
    for k, o in enumerate((d0, d1, d2, d3)):
        o[...] = dg(dlow, wo[k], NN).astype(bf16)


def grad_fc_kernel(
    place, du, h2, da, a0, a1, a2, a3, s0, s1, k0, k1, wide, narrow,
):
    b, s = place[0], place[1]
    outs = ((k0, k1), (s0, s1))
    for m in range(FB):
        z = (b // 2) ^ (m // 2)
        wide[...] = dg(h2[...], du[b ^ m], TN).astype(bf16)
        for k in range(PARTS):
            outs[k % 2][k // 2][m % 2, z, 0:ROWS, :] = wide[
                pl.ds(pl.multiple_of((s ^ k) * ROWS, 16), ROWS), :
            ]
    for k, a in enumerate((a0, a1, a2, a3)):
        narrow[...] = dg(da[...], a[...], TN).astype(bf16)
        for m in range(FB):
            z = (b // 2) ^ (m // 2)
            for i in range(2):
                outs[k % 2][k // 2][m % 2, z, ROWS:, i * GROUP : (i + 1) * GROUP] = narrow[
                    pl.ds(pl.multiple_of((b ^ m) * DB + i * HALF, 16), HALF), :
                ]


def grad_proj_kernel(place, act, dm, send0, send1, keep0, keep1, wide):
    b, s = place[0], place[1]
    for k in range(PARTS):
        outs = (send0, send1) if k % 2 else (keep0, keep1)
        for j in range(2):
            wide[...] = dg(dm[...], act[2 * (s ^ k) + j], TN).astype(bf16)
            for m in range(FB):
                outs[m % 2][(b // 2) ^ (m // 2), k // 2, j * DB : (j + 1) * DB, :] = wide[
                    pl.ds(pl.multiple_of((b ^ m) * DB, 16), DB), :
                ]


def arrange_kernel(place, g0, g1, g2, g3, send, keep, whole):
    b, s = place[0], place[1]
    tail = jnp.zeros((2 * FB, ROWS), f32)
    for k, g in enumerate((g0, g1, g2, g3)):
        for p in range(3):
            at = pl.multiple_of(p * D + (s ^ k) * GROUP, 16)
            whole[pl.ds(at, GROUP), :] = g[p * GROUP : (p + 1) * GROUP, :]
        tail = tail + g[3 * GROUP :, :].astype(f32)
    for m in range(FB):
        out = send if m % 2 else keep
        for i in range(2):
            half = slice(i * ROWS, (i + 1) * ROWS)
            out[m // 2, 0:QH, half] = whole[
                pl.ds(pl.multiple_of((b ^ m) * QB + i * QH, 16), QH), :
            ]
            row = tail[2 * m + i : 2 * m + i + 1, :]
            extra = jnp.concatenate([row, jnp.zeros((7, ROWS), f32)], 0)
            out[m // 2, QH:, half] = extra.astype(bf16)


def adam_refs(refs, outs, grad, rate, decay):
    for out, value in zip(outs, adam_update(*(r[...] for r in refs), grad, rate, decay)):
        out[...] = value


def adam_q_kernel(place, p0, p1, p2, p3, *refs):
    total = (p0[...].astype(f32) + p1[...].astype(f32)) + (
        p2[...].astype(f32) + p3[...].astype(f32)
    )
    grad = jnp.concatenate([total[0:QH, 0:ROWS].T, total[0:QH, ROWS:].T], 1)
    adam_refs(refs[0:3], refs[6:10], grad, D ** (-0.5), matrix_decay)
    row = total[QH : QH + 1, :]
    vec = jnp.concatenate([row[:, i * DB : (i + 1) * DB] for i in range(3)], 0)
    adam_refs(refs[3:6], refs[10:14], vec, 0.5, 0.0)


def adam_a_kernel(place, p0, p1, p2, p3, *refs):
    total = (p0[...].astype(f32) + p1[...].astype(f32)) + (
        p2[...].astype(f32) + p3[...].astype(f32)
    )
    adam_refs(refs[0:3], refs[6:10], total[0:ROWS, :], D ** (-0.5), matrix_decay)
    grad = jnp.concatenate([total[ROWS:, 0:GROUP].T, total[ROWS:, GROUP:].T], 1)
    adam_refs(refs[3:6], refs[10:14], grad, max(1, 16 * D // LEN) ** (-0.5), matrix_decay)


def adam_b_kernel(place, mine, got, *refs):
    total = mine[...] + got[...].astype(f32)
    grad = jnp.concatenate([total[0:DB, :].T, total[DB:, :].T], 0)
    adam_refs(refs[0:3], refs[3:7], grad, FF ** (-0.5), matrix_decay)


def last_kernel(place, dx1, own, other, x, vec, out):
    hat, scale = norm_parts(x[...].astype(f32))
    e = (own[...].astype(f32) + other[...].astype(f32)) * vec[0:1, :]
    back = scale * (e - jnp.mean(e, -1, keepdims=True) - hat * jnp.mean(e * hat, -1, keepdims=True))
    out[...] = (dx1[...] + back).astype(bf16)


def local(
    inputs, cotangent,
    qkv_weight, qkv_first, qkv_second,
    out_weight, out_first, out_second,
    fc_weight, fc_first, fc_second,
    proj_weight, proj_first, proj_second,
    vectors, vector_first, vector_second,
):
    dp = lax.axis_size("dp")
    by_pairs = dp == FB
    b = lax.axis_index("dp").astype(jnp.int32)
    s = lax.axis_index("seq").astype(jnp.int32)
    place = jnp.stack([b if by_pairs else jnp.zeros_like(b), s])
    split = dp // FB

    x = [inputs.reshape(TOK, D)]
    cot = cotangent.reshape(TOK, D)
    x.append(swap(x[0], "seq", 1))
    x.append(swap(x[0], "seq", 2))

    low_qkv = qkv_weight.astype(bf16).T
    low_vec = vectors.astype(bf16)
    low_fc = fc_weight.astype(bf16)
    low_proj = proj_weight.astype(bf16).T
    low_out = out_weight.astype(bf16).T

    def call(kernel, args, outs, scratch, cost, name, spare=4, deps=()):
        return list(vmem_call(kernel, [place, *args], outs, scratch, cost, name, spare, deps))

    def with_vec(weight, value):
        n = weight.shape[0]
        weight = jnp.concatenate([weight[:, :QH], weight[:, QH:]], 2)
        row = jnp.pad(value.reshape(n, 1, 3 * DB), ((0, 0), (0, 7), (0, DB)))
        return jnp.concatenate([weight, row], 1)

    def as_late(fc, proj, out):
        n = fc.shape[0]
        out = out.reshape(n, 2, HALF, ROWS).transpose(0, 2, 1, 3).reshape(n, HALF, FC)
        proj = proj.reshape(n, DB, 2, FC).transpose(0, 2, 1, 3).reshape(n, ROWS, FC)
        return jnp.concatenate([fc, out], 1), proj

    def pairs_first(value):
        return value.reshape((4, 2) + value.shape[1:]).swapaxes(0, 1)

    if by_pairs:
        mine = with_vec(low_qkv[None], low_vec[None])[0]
        late = jnp.concatenate(as_late(low_fc[None], low_proj[None], low_out[None]), 1)[0]
        z_qkv = call(
            stack_kernel, direct([mine] * 4), [shape((4, QP, 2 * ROWS), bf16)], [], 1, "stack_qkv"
        )[0]
        z_qkv, x[2] = tie(z_qkv, x[2])
        x.append(swap(x[2], "seq", 1))
        x_qkv = swap(z_qkv, "dp", 1)
        groups = [[2 * z + i for z in range(4)] for i in range(2)]
        line = lax.all_gather(late, "dp", axis_index_groups=groups)
        line, x_qkv = tie(line, x_qkv)
        line = (line[:, :AR], line[:, AR:])
    else:
        x.append(swap(x[2], "seq", 1))
        all_qkv = lax.all_gather(low_qkv, "dp").reshape(FB, QB, ROWS)
        all_vec = lax.all_gather(low_vec, "dp").transpose(1, 0, 2).reshape(3, FB, DB)
        z_qkv, x_qkv = pairs_first(with_vec(all_qkv, all_vec.transpose(1, 0, 2)))
        all_fc = lax.all_gather(low_fc, "dp").reshape(FB, split, ROWS, FC // split)
        all_fc = all_fc.transpose(0, 2, 1, 3).reshape(FB, ROWS, FC)
        all_proj = lax.all_gather(low_proj, "dp").reshape(FB, DB, D)
        all_out = lax.all_gather(low_out, "dp").reshape(FB, DB, ROWS)
        all_a, all_b = as_late(all_fc, all_proj, all_out)
        late_parts = []
        for part in (all_a, all_b):
            own = pairs_first(part)
            other = swap(own, "seq", 2)
            late_parts.append([own[0], own[1], other[0], other[1]])

    x_qkv, x[1], x[3] = tie(x_qkv, x[1], x[3])
    group_shape = shape((3 * GROUP + 2 * FB, ROWS), bf16)
    picked = call(
        pick_kernel, [z_qkv, x_qkv], [group_shape] * PARTS, [pltpu.VMEM((3 * D, ROWS), bf16)],
        2, "pick",
    )
    wq = seq_exchange(picked)
    if by_pairs:
        own_y, wq[2], wq[3] = tie(line, wq[2], wq[3])
        x_b, x_a = swap(line[1], "dp", 1), swap(line[0], "dp", 1)
        y_b, y_a = swap(own_y[1], "seq", 2), swap(own_y[0], "seq", 2)
        first_deps = [x_b]
    else:
        first_deps = []

    def both_cores(parts):
        return [w for p in parts for w in (p, swap(p, "seq", 1))]

    lse_shape = shape((1, LEN), f32)
    head_shape = shape((LEN, HEAD_DIM), bf16)
    head_space = [pltpu.VMEM((LEN, HEAD_DIM), bf16)]
    qkv0, qkv1, qkv2, wt, head0, lse0, vec, fbias = call(
        first_kernel, [*x, *wq],
        [shape((3, LEN, HEAD_DIM), bf16)] * OWN_HEADS
        + [shape((3 * GROUP, D), bf16), head_shape, lse_shape]
        + [shape((12, D), f32), shape((FB, 1, FC), f32)],
        [pltpu.VMEM((PARTS, 3 * GROUP, ROWS), bf16), pltpu.VMEM((PARTS, FB, 3, DB), f32)], 16, "first", 14,
        deps=first_deps,
    )
    head1, lse1 = call(second_kernel, [qkv1], [head_shape, lse_shape], [], 2, "second", 14)
    if by_pairs:
        y_b, head1 = tie(y_b, head1)
        late_b = [line[1], x_b, y_b, swap(y_b, "dp", 1)]
    *at, lse2 = call(
        third_kernel, [qkv2, head0, head1], [shape((TOK, GROUP), bf16)] * PARTS + [lse_shape],
        head_space, 7, "third", 14,
    )
    if by_pairs:
        y_a, lse2 = tie(y_a, lse2)
        late_parts = [[line[0], x_a, y_a, swap(y_a, "dp", 1)], late_b]
    rows = seq_exchange(at)
    late_a, late_b, rows[1], rows[2], rows[3] = tie(*late_parts, *rows[1:])
    heads = ((qkv0, lse0), (qkv1, lse1), (qkv2, lse2))

    mid_shape = shape((TOK, D), f32)
    wide_shape = shape((FB, TOK, FC), bf16)
    out, act, du, h2, dm, da, dx1, d0, d1, d2, d3, gvec, gfb = call(
        middle_kernel, [*rows, x[0], cot, *both_cores(late_a), *both_cores(late_b), vec, fbias],
        [shape((TOK, D), bf16), wide_shape, wide_shape]
        + [shape((TOK, D), bf16)] * 3 + [mid_shape] + [shape((TOK, GROUP), bf16)] * PARTS
        + [shape((4, D), f32), shape((FB, 1, FC), f32)],
        [pltpu.VMEM((PARTS, D, GROUP), bf16), pltpu.VMEM((D, FC), bf16), pltpu.VMEM((D, FC), bf16),
         pltpu.VMEM((TOK, D), f32), pltpu.VMEM((TOK, D), f32), pltpu.VMEM((TOK, D), f32)],
        28, "middle", 10,
    )
    gout = seq_exchange([d0, d1, d2, d3])

    def fold(keep, got, name, deps=()):
        flat = [v.reshape((-1,) + v.shape[-2:]) for v in (*keep, *got)]
        outs = call(
            fold_kernel, flat, [shape(f.shape, bf16) for f in flat[: len(keep)]], [], 2, name, 4,
            deps,
        )
        return [o.reshape(k.shape) for o, k in zip(outs, keep)]


    *a_send, a0, a1 = call(
        grad_fc_kernel, [du, h2, da, *rows], [shape((2, 4, AR, FC), bf16)] * 4,
        [pltpu.VMEM((D, FC), bf16), pltpu.VMEM((D, GROUP), bf16)], 0.3, "grad_fc",
    )
    a_got = [swap(p, "seq", 1) for p in a_send]
    *b_send, b0, b1 = call(
        grad_proj_kernel, [act, dm],
        [shape((4, 2, ROWS, FC), bf16)] * 4, [pltpu.VMEM((D, FC), bf16)], 0.3, "grad_proj",
        deps=[a0],
    )
    b_got = [swap(p, "seq", 1) for p in b_send]

    def backward(h, cost, deps):
        qkv, lse = heads[h]
        return call(
            functools.partial(backward_kernel, head=h),
            [qkv, *gout, *at, lse], [shape((3, LEN, HEAD_DIM), bf16)],
            [pltpu.VMEM((LEN, HEAD_DIM), bf16), pltpu.VMEM((LEN, 1), f32),
             pltpu.VMEM((HEAD_DIM, LEN), f32), pltpu.VMEM((HEAD_DIM, LEN), f32)],
            cost, "backward", 14, deps=deps,
        )[0]

    def plain(mine):
        return lax.psum_scatter(mine, "dp", scatter_dimension=0, tiled=False).astype(f32)

    back0 = backward(0, 36, [b0])
    a_mine, a_other = fold([a0, a1], a_got, "fold_a_core", [back0])
    b_mine, b_other = fold([b0, b1], b_got, "fold_b_core", [a_mine])
    back1 = backward(1, 6, [b_mine])
    back2 = backward(2, 6, [back1])
    dk0, dk1, ds0, ds1, *gq = call(
        gather_kernel, [back0, back1, back2, wt, *x, vec, gvec, gfb],
        [shape((TOK, D), bf16)] * 4 + [group_shape] * PARTS,
        [pltpu.VMEM((3 * GROUP, D), f32), pltpu.VMEM((PARTS, 3 * GROUP, ROWS), bf16),
         pltpu.VMEM((PARTS, 1, 3 * GROUP), f32), pltpu.VMEM((PARTS, FB, 3, DB), f32)],
        3, "gather", 8,
    )
    gq = seq_exchange(gq)
    if by_pairs:
        b_pieces = call(
            line_kernel, [b_mine, swap(b_other, "dp", 1)], [shape((2, ROWS, FC), bf16)] * 4,
            [], 1, "fold_b_x", deps=[gq[1]],
        )
        a_mine, a_other = call(
            split_kernel, [a_mine, swap(a_other, "seq", 2)], [shape((4, AR, FC), bf16)] * 2,
            [], 1, "fold_a_y", deps=[b_pieces[0]],
        )
        b_pieces = direct(b_pieces)
        q_deps = [a_mine, b_pieces[2]]
    else:
        q_deps = []
    q_send, q_keep = call(
        arrange_kernel, gq, [shape((4, QP, 2 * ROWS), bf16)] * 2,
        [pltpu.VMEM((3 * D, ROWS), bf16)], 2, "arrange", deps=q_deps,
    )
    if by_pairs:
        q_pieces = call(
            pieces_kernel, [q_keep, swap(q_send, "dp", 1)],
            [shape((QP, 2 * ROWS), bf16)] * 4, [], 2, "fold_q_x",
        )
        q_pieces[0], ds0, ds1 = tie(q_pieces[0], ds0, ds1)
        q_pieces = direct(q_pieces)
        proj, proj_send = call(
            four_kernel, b_pieces, [shape((ROWS, FC), f32), shape((ROWS, FC), bf16)],
            [], 1, "sum_b", deps=[q_pieces[0]],
        )
        a_pieces = call(
            line_kernel, [a_mine, swap(a_other, "dp", 1)], [shape((AR, FC), bf16)] * 4,
            [], 1, "fold_a_x", deps=[proj_send],
        )
        dh_deps = [a_pieces[0]]
        a_pieces = direct(a_pieces)
        proj_got = swap(proj_send, "seq", 2)
    else:
        dh_deps = []

        def flat(mine):
            return mine.swapaxes(0, 1).reshape((FB,) + mine.shape[2:])

        a_got = swap(a_other, "seq", 2)
        all_a = flat(fold([a_mine], [a_got], "fold_a_y")[0])
        b_mine = [p[:, 0] for p in (b_mine, b_other)], [p[:, 1] for p in (b_mine, b_other)]
        b_got = [swap(p, "seq", 2) for p in b_mine[1]]
        all_b = flat(jnp.stack(fold(b_mine[0], b_got, "fold_b_y")))
        fc = all_a[:, :ROWS].reshape(FB, ROWS, split, FC // split).transpose(0, 2, 1, 3)
        sum_fc = plain(fc.reshape(dp, ROWS, FC // split))
        go = all_a[:, ROWS:].reshape(FB, HALF, 2, ROWS).transpose(0, 2, 1, 3)
        sum_out = plain(go.reshape(dp, D // dp, ROWS)).T
        proj = all_b.reshape(FB, 2, DB, FC).transpose(0, 2, 1, 3)
        sum_proj = plain(proj.reshape(dp, D // dp, D)).T
        all_q = flat(jnp.stack([q_keep, q_send]))
        halves = [all_q[:, :QH, :ROWS], all_q[:, :QH, ROWS:]]
        sum_qkv = plain(jnp.concatenate(halves, 1).reshape(dp, 3 * D // dp, ROWS)).T
        vrows = all_q[:, QH].reshape(FB, 4, DB)[:, :3]
        vrows = vrows.reshape(FB, 3, split, DB // split).transpose(0, 2, 1, 3)
        sum_vec = plain(vrows.reshape(dp, 3, DB // split))
    own, other = fold([dk0, dk1], [swap(ds0, "seq", 1), swap(ds1, "seq", 1)], "fold_dh", dh_deps)
    other = swap(other, "seq", 2)

    (input_grad,) = call(
        last_kernel, [dx1, own, other, x[0], vec], [shape((TOK, D), bf16)], [], 4, "last"
    )

    qkv_set = (qkv_weight, qkv_first, qkv_second)
    out_set = (out_weight, out_first, out_second)
    fc_set = (fc_weight, fc_first, fc_second)
    proj_set = (proj_weight, proj_first, proj_second)
    vec_set = (vectors, vector_first, vector_second)
    if by_pairs:

        def news(group):
            return [shape(group[0].shape, d) for d in (f32, f32, f32, bf16)]

        new = call(
            adam_q_kernel, [*q_pieces, *qkv_set, *vec_set], news(qkv_set) + news(vec_set),
            [], 3, "adam_qkv",
        )
        qkv_new, vec_new = new[:4], new[4:]
        new = call(
            adam_a_kernel, [*a_pieces, *fc_set, *out_set], news(fc_set) + news(out_set),
            [], 3, "adam_fc",
        )
        fc_new, out_new = new[:4], new[4:]
        proj_new = call(
            adam_b_kernel, [proj, proj_got, *proj_set], news(proj_set), [], 3, "adam_proj"
        )
    else:
        qkv_new = adam_update(*qkv_set, sum_qkv, D ** (-0.5), matrix_decay)
        out_new = adam_update(*out_set, sum_out, max(1, 16 * D // LEN) ** (-0.5), matrix_decay)
        fc_new = adam_update(*fc_set, sum_fc, D ** (-0.5), matrix_decay)
        proj_new = adam_update(*proj_set, sum_proj, FF ** (-0.5), matrix_decay)
        vec_new = adam_update(*vec_set, sum_vec, 0.5, 0.0)
    return (
        out.reshape(inputs.shape),
        input_grad.reshape(inputs.shape),
        *qkv_new,
        *out_new,
        *fc_new,
        *proj_new,
        *vec_new,
    )


def solution(mesh):
    rows = P("dp", "seq", None)
    block = P("seq", "dp")
    return jax.shard_map(
        local,
        mesh=mesh,
        in_specs=(rows, rows) + (block,) * 15,
        out_specs=(rows, rows) + (block,) * 20,
        check_vma=False,
    )
```

```python
import functools

import jax
import jax.numpy as jnp
from jax import lax
from jax.experimental import pallas as pl
from jax.experimental.pallas import tpu as pltpu
from jax.sharding import PartitionSpec as P

D = 768
HEADS = 12
HEAD_DIM = 64
FF = 3072
DEPTH = 12
LEN = 2048
STEP = 10
PARTS = 4
TOK = LEN // PARTS
OWN_HEADS = HEADS // PARTS
GROUP = OWN_HEADS * HEAD_DIM
ROWS = D // PARTS
FB = 8
FC = FF // FB
DB = D // FB
QB = 3 * D // FB
QH = QB // 2
QP = QH + 8
HALF = DB // 2
AR = ROWS + HALF
LR = AR + ROWS
BRANCH = DEPTH ** (-0.5)
EPS = 1e-05

beta_one = 0.5
beta_two = 0.5
matrix_decay = 0.1

f32 = jnp.float32
bf16 = jnp.bfloat16

NN = (((1,), (0,)), ((), ()))
NT = (((1,), (1,)), ((), ()))
TN = (((0,), (0,)), ((), ()))


def dg(left, right, dims):
    return lax.dot_general(left, right, dims, preferred_element_type=f32)


def adam_update(master, first, second, grad, rate, decay):
    first_new = beta_one * first + (1.0 - beta_one) * grad
    second_new = beta_two * second + (1.0 - beta_two) * grad * grad
    fix_one = 1.0 - beta_one**STEP
    fix_two = 1.0 - beta_two**STEP
    direction = first_new / fix_one / (jnp.sqrt(second_new / fix_two) + 1e-08)
    updated = master - rate * (direction + decay * master)
    return (first_new, second_new, updated, updated.astype(bf16))


def swap(value, axis, k):
    n = lax.axis_size(axis)
    return lax.ppermute(value, axis, [(i, i ^ k) for i in range(n)])


def direct(pieces):
    return [pieces[0]] + [swap(pieces[k], "dp", 2 * k) for k in (1, 2, 3)]


def seq_exchange(values):
    return [values[0]] + [swap(values[k], "seq", k) for k in range(1, PARTS)]


def z_exchange(value):
    groups = [[2 * z + x for z in range(4)] for x in range(2)]
    return lax.all_to_all(value, "dp", 0, 0, axis_index_groups=groups, tiled=True)


def tie(*values):
    return lax.optimization_barrier(values)


VM = pl.BlockSpec(memory_space=pltpu.VMEM)
SM = pl.BlockSpec(memory_space=pltpu.SMEM)


def space(item):
    dims = list(item.shape)
    dims[-1] = -(-dims[-1] // 128) * 128
    if len(dims) > 1:
        dims[-2] = -(-dims[-2] // 8) * 8
    size = jnp.dtype(item.dtype).itemsize
    for d in dims:
        size *= d
    return size


def vmem_call(kernel, args, outs, scratch, flops, name, spare=4, deps=()):
    n = len(args)

    def body(*refs):
        kernel(*refs[:n], *refs[n + len(deps) :])

    need = sum(space(a) for a in (*args[1:], *outs, *scratch)) + spare * 2**20
    return pl.pallas_call(
        body,
        out_shape=tuple(outs),
        in_specs=[SM] + [VM] * (n - 1) + [pl.BlockSpec(memory_space=pl.ANY)] * len(deps),
        out_specs=tuple([VM] * len(outs)),
        scratch_shapes=list(scratch),
        compiler_params=pltpu.CompilerParams(vmem_limit_bytes=need),
        cost_estimate=pl.CostEstimate(
            flops=int(flops * 0.5e9), bytes_accessed=1024, transcendentals=0
        ),
        name=name,
    )(*args, *deps)


def shape(dims, dtype):
    return jax.ShapeDtypeStruct(dims, dtype)


def norm_parts(values):
    centre = values - jnp.mean(values, -1, keepdims=True)
    spread = jnp.mean(centre * centre, -1, keepdims=True)
    scale = lax.rsqrt(spread + EPS)
    return centre * scale, scale


def stack_kernel(place, p0, p1, p2, p3, out):
    for k, p in enumerate((p0, p1, p2, p3)):
        out[k] = p[...]


def place_kernel(place, p, a, b):
    for k in range(4):
        a[k] = p[k, 0:AR, :]
        b[k] = p[k, AR:, :]


def pick_kernel(place, z, x, o0, o1, o2, o3, whole):
    b, s = place[0], place[1]
    for m in range(FB):
        part = (z, x)[m % 2]
        for i in range(2):
            whole[pl.ds(pl.multiple_of((b ^ m) * QB + i * QH, 16), QH), :] = part[
                m // 2, 0:QH, i * ROWS : (i + 1) * ROWS
            ]
    tail = jnp.concatenate(
        [
            (z, x)[m % 2][m // 2, QH : QH + 1, i * ROWS : (i + 1) * ROWS]
            for m in range(FB)
            for i in range(2)
        ],
        0,
    )
    for k, out in enumerate((o0, o1, o2, o3)):
        for p in range(3):
            at = pl.multiple_of(p * D + (s ^ k) * GROUP, 16)
            out[p * GROUP : (p + 1) * GROUP, :] = whole[pl.ds(at, GROUP), :]
        out[3 * GROUP :, :] = tail


def fold_kernel(place, *refs):
    n = len(refs) // 3
    for keep, got, out in zip(refs[:n], refs[n : 2 * n], refs[2 * n :]):

        def step(j, _):
            out[j] = (keep[j].astype(f32) + got[j].astype(f32)).astype(bf16)
            return 0

        lax.fori_loop(0, keep.shape[0], step, 0)


def pieces_kernel(place, keep, got, *outs):
    for k, out in enumerate(outs):
        out[...] = (keep[k].astype(f32) + got[k].astype(f32)).astype(bf16)


def split_kernel(place, keep, got, mine, other):
    def step(j, _):
        for i, out in enumerate((mine, other)):
            out[j] = (keep[i, j].astype(f32) + got[i, j].astype(f32)).astype(bf16)
        return 0

    lax.fori_loop(0, keep.shape[1], step, 0)


def line_kernel(place, keep, got, *outs):
    for k, out in enumerate(outs):
        j = (place[0] // 2) ^ k
        out[...] = (keep[j].astype(f32) + got[j].astype(f32)).astype(bf16)


def four_kernel(place, p0, p1, p2, p3, mine, other):
    for i, out in enumerate((mine, other)):
        total = (p0[i].astype(f32) + p1[i].astype(f32)) + (p2[i].astype(f32) + p3[i].astype(f32))
        out[...] = total.astype(out.dtype)


def attend(qkv, lse, heads_out):
    for i in range(PARTS):
        qi = qkv[0, i * TOK : (i + 1) * TOK, :]
        n = (i + 1) * TOK
        sc = dg(qkv[1, 0:n, :], qi, NT)
        kp = lax.broadcasted_iota(jnp.int32, (TOK, TOK), 0)
        qp = lax.broadcasted_iota(jnp.int32, (TOK, TOK), 1)
        last = jnp.where(kp <= qp, sc[i * TOK :], -1e30)
        mx = jnp.max(last, 0, keepdims=True)
        if i:
            mx = jnp.maximum(mx, jnp.max(sc[: i * TOK], 0, keepdims=True))
        e_last = jnp.exp(last - mx)
        total = jnp.sum(e_last, 0, keepdims=True)
        e = e_last.astype(bf16)
        if i:
            e_first = jnp.exp(sc[: i * TOK] - mx)
            total = total + jnp.sum(e_first, 0, keepdims=True)
            e = jnp.concatenate([e_first.astype(bf16), e], 0)
        o = dg(qkv[2, 0:n, :], e, TN) / total
        heads_out[i * TOK : (i + 1) * TOK, :] = o.T.astype(bf16)
        lse[:, i * TOK : (i + 1) * TOK] = mx + jnp.log(total)


def first_kernel(
    place, x0, x1, x2, x3, w0, w1, w2, w3,
    qkv0, qkv1, qkv2, wt, heads_out, lse, vec, fbias, pieces, blocks,
):
    b, s = place[0], place[1]
    for k, w in enumerate((w0, w1, w2, w3)):
        pieces[s ^ k] = w[0 : 3 * GROUP, :]
        tail = w[3 * GROUP :, :].astype(f32)
        for m in range(FB):
            blocks[s ^ k, b ^ m, 0:1, :] = tail[2 * m : 2 * m + 1, 0:DB]
            blocks[s ^ k, b ^ m, 1:2, :] = tail[2 * m : 2 * m + 1, DB : 2 * DB]
            blocks[s ^ k, b ^ m, 2:3, :] = tail[2 * m + 1 : 2 * m + 2, 0:DB]
    for j in range(PARTS):
        wt[:, j * ROWS : (j + 1) * ROWS] = pieces[j]
    qbias = jnp.zeros((1, GROUP), f32)
    vbias = jnp.zeros((1, GROUP), f32)
    for r in range(12):
        row = jnp.concatenate([blocks[r // 3, m, r % 3 : r % 3 + 1, :] for m in range(FB)], 1)
        vec[r : r + 1, :] = row
        for m in range(PARTS):
            mine = row[:, m * GROUP : (m + 1) * GROUP]
            if r == 2:
                qbias = jnp.where(s == m, mine, qbias)
            if r == 3:
                vbias = jnp.where(s == m, mine, vbias)
        for m in range(2):
            if r >= 8:
                fbias[2 * (r - 8) + m] = row[:, m * FC : (m + 1) * FC]
    bias = jnp.concatenate([qbias, jnp.zeros((1, GROUP), f32), vbias], 1)
    for k, x in enumerate((x0, x1, x2, x3)):
        rows = pl.ds(pl.multiple_of((s ^ k) * TOK, TOK), TOK)
        hat, _ = norm_parts(x[...].astype(f32))
        h = (hat * vec[0:1, :] + vec[1:2, :]).astype(bf16)
        r = (dg(h, wt[...], NT) + bias).astype(bf16)
        for i in range(3 * OWN_HEADS):
            part = r[:, i * HEAD_DIM : (i + 1) * HEAD_DIM]
            if i < OWN_HEADS:
                part = (part.astype(f32) * HEAD_DIM ** (-0.5)).astype(bf16)
            (qkv0, qkv1, qkv2)[i % OWN_HEADS][i // OWN_HEADS, rows, :] = part
    attend(qkv0, lse, heads_out)


def second_kernel(place, qkv, heads_out, lse):
    attend(qkv, lse, heads_out)


def third_kernel(place, qkv, head0, head1, at0, at1, at2, at3, lse, head2):
    s = place[1]
    attend(qkv, lse, head2)
    for k, at in enumerate((at0, at1, at2, at3)):
        rows = pl.ds(pl.multiple_of((s ^ k) * TOK, TOK), TOK)
        for i, head in enumerate((head0, head1, head2)):
            at[:, i * HEAD_DIM : (i + 1) * HEAD_DIM] = head[rows, :]


def backward_kernel(
    place, qkv, g0, g1, g2, g3, at0, at1, at2, at3, lse,
    dheads, gout, delta, dkt, dvt, *, head,
):
    s = place[1]
    lanes = slice(head * HEAD_DIM, (head + 1) * HEAD_DIM)
    for k, (g, at) in enumerate(zip((g0, g1, g2, g3), (at0, at1, at2, at3))):
        rows = pl.ds(pl.multiple_of((s ^ k) * TOK, TOK), TOK)
        gv = g[:, lanes]
        gout[rows, :] = gv
        delta[rows, :] = jnp.sum(gv.astype(f32) * at[:, lanes].astype(f32), 1, keepdims=True)
    for i in range(PARTS):
        cut = slice(i * TOK, (i + 1) * TOK)
        qi = qkv[0, cut, :]
        gi = gout[cut, :]
        di = delta[cut, :]
        li = lse[:, cut].T
        dq = jnp.zeros((TOK, HEAD_DIM), f32)
        for j in range(i + 1):
            keys = slice(j * TOK, (j + 1) * TOK)
            kj = qkv[1, keys, :]
            vj = qkv[2, keys, :]
            sc = dg(qi, kj, NT)
            if j == i:
                qp = lax.broadcasted_iota(jnp.int32, (TOK, TOK), 0)
                kp = lax.broadcasted_iota(jnp.int32, (TOK, TOK), 1)
                sc = jnp.where(kp <= qp, sc, -1e30)
            p = jnp.exp(sc - li)
            dp = dg(gi, vj, NT)
            ds = (p * (dp - di)).astype(bf16)
            dq = dq + dg(ds, kj, NN)
            dv = dg(gi, p.astype(bf16), TN)
            dk = dg(qi, ds, TN)
            if j == i:
                dkt[:, keys] = dk
                dvt[:, keys] = dv
            else:
                dkt[:, keys] += dk
                dvt[:, keys] += dv
        dheads[0, cut, :] = (dq * HEAD_DIM ** (-0.5)).astype(bf16)
    for j in range(PARTS):
        keys = slice(j * TOK, (j + 1) * TOK)
        dheads[1, keys, :] = dkt[:, keys].T.astype(bf16)
        dheads[2, keys, :] = dvt[:, keys].T.astype(bf16)


def gather_kernel(
    place, e0, e1, e2, wt, x0, x1, x2, x3, vec, gvec, gfb,
    dk0, dk1, ds0, ds1, gq0, gq1, gq23, gsum, gpieces, gbias, rows_of,
):
    b, s = place[0], place[1]
    gsum[...] = jnp.zeros_like(gsum)
    sums = jnp.zeros((1, 3 * GROUP), f32)
    gain = jnp.zeros((1, D), f32)
    shift = jnp.zeros((1, D), f32)
    for k, x in enumerate((x0, x1, x2, x3)):
        rows = pl.ds(pl.multiple_of((s ^ k) * TOK, TOK), TOK)
        dqkv = jnp.concatenate([e[i, rows, :] for i in range(3) for e in (e0, e1, e2)], 1)
        hat, _ = norm_parts(x[...].astype(f32))
        h = (hat * vec[0:1, :] + vec[1:2, :]).astype(bf16)
        gsum[...] += dg(dqkv, h, TN)
        sums = sums + jnp.sum(dqkv.astype(f32), 0, keepdims=True)
        part = dg(dqkv, wt[...], NN)
        (dk0, ds0, dk1, ds1)[k][...] = part.astype(bf16)
        gain = gain + jnp.sum(part * hat, 0, keepdims=True)
        shift = shift + jnp.sum(part, 0, keepdims=True)
    for m in range(PARTS):
        gpieces[m] = gsum[:, m * ROWS : (m + 1) * ROWS].astype(bf16)
    outs = (
        (gq0, slice(0, ROWS)),
        (gq1, slice(0, ROWS)),
        (gq23, slice(0, ROWS)),
        (gq23, slice(ROWS, 2 * ROWS)),
    )
    for k, (out, lanes) in enumerate(outs):
        out[0 : 3 * GROUP, lanes] = gpieces[s ^ k]
    gbias[...] = jnp.zeros_like(gbias)
    gbias[s] = sums
    qrow = jnp.concatenate([gbias[m, :, 0:GROUP] for m in range(PARTS)], 1)
    vrow = jnp.concatenate([gbias[m, :, 2 * GROUP : 3 * GROUP] for m in range(PARTS)], 1)
    for r in range(12):
        if r < 4:
            row = (gain, shift, qrow, vrow)[r]
        elif r < 8:
            row = gvec[r - 4 : r - 3, :]
        else:
            row = jnp.concatenate([gfb[2 * (r - 8)], gfb[2 * (r - 8) + 1]], 1)
        for m in range(FB):
            rows_of[r // 3, m, r % 3 : r % 3 + 1, :] = row[:, m * DB : (m + 1) * DB]
    for k, (out, lanes) in enumerate(outs):
        tail = []
        for m in range(FB):
            part = rows_of[s ^ k, b ^ m]
            tail.append(jnp.concatenate([part[0:1, :], part[1:2, :]], 1))
            tail.append(jnp.concatenate([part[2:3, :], jnp.zeros((1, DB), f32)], 1))
        out[3 * GROUP :, lanes] = jnp.concatenate(tail, 0).astype(bf16)


def middle_kernel(
    place, a0, a1, a2, a3, x, cot, l0, l1, l2, l3, l4, l5, l6, l7,
    p0, p1, p2, p3, p4, p5, p6, p7, vec, fbias,
    out, act, du, h2, dm, da, dx1, d0, d1, d2, d3, gvec, gfb, wo, wf, wp, mid, macc, dacc,
):
    b, s = place[0], place[1]
    weights = (l0, l1, l2, l3, l4, l5, l6, l7)
    downs = (p0, p1, p2, p3, p4, p5, p6, p7)
    for k in range(PARTS):
        for m in range(FB):
            low = weights[4 * (k // 2) + 2 * (m % 2) + k % 2]
            for i in range(2):
                wo[k, pl.ds(pl.multiple_of((b ^ m) * DB + i * HALF, 16), HALF), :] = low[
                    (b // 2) ^ (m // 2), ROWS:AR, i * GROUP : (i + 1) * GROUP
                ]
    proj = dg(a0[...], wo[0], NT)
    for k, a in ((1, a1), (2, a2), (3, a3)):
        proj = proj + dg(a[...], wo[k], NT)
    x1 = x[...].astype(f32) + BRANCH * (proj + vec[4:5, :])
    mid[...] = x1
    hat, _ = norm_parts(x1)
    h2[...] = (hat * vec[5:6, :] + vec[6:7, :]).astype(bf16)
    low = (BRANCH * cot[...].astype(f32)).astype(bf16)
    dm[...] = low
    gvec[3:4, :] = jnp.sum(low.astype(f32), 0, keepdims=True)
    macc[...] = jnp.zeros_like(macc)
    dacc[...] = jnp.zeros_like(dacc)

    def chunk(z, _, q):
        j = (b % 2) ^ q
        f = 2 * z + j
        for m in range(PARTS):
            part = weights[4 * (m // 2) + 2 * q + m % 2]
            wf[pl.ds(pl.multiple_of((s ^ m) * ROWS, 16), ROWS), :] = part[z, 0:ROWS, :]
        for k in range(PARTS):

            @pl.when((s ^ z) == k)
            def _():
                for m in range(FB):
                    part = downs[4 * (k // 2) + 2 * (m % 2) + k % 2]
                    wp[pl.ds(pl.multiple_of((b ^ m) * DB, 16), DB), :] = part[
                        (b // 2) ^ (m // 2), pl.ds(pl.multiple_of(j * DB, 16), DB), :
                    ]

        u = dg(h2[...], wf[...], NN) + fbias[f]
        coef = (2.0 / jnp.pi) ** 0.5
        th = jnp.tanh(coef * (u + 0.044715 * (u * u * u)))
        half = 0.5 * (1.0 + th)
        av = (u * half).astype(bf16)
        act[f] = av
        slope = half + 0.5 * u * (1.0 - th * th) * (coef * (1.0 + 3 * 0.044715 * (u * u)))
        dv = (dg(dm[...], wp[...], NN) * slope).astype(bf16)
        du[f] = dv
        gfb[f] = jnp.sum(dv.astype(f32), 0, keepdims=True)
        macc[...] += dg(av, wp[...], NT)
        dacc[...] += dg(dv, wf[...], NT)
        return 0

    for q in range(2):
        lax.fori_loop(0, 4, functools.partial(chunk, q=q), 0)
    x1 = mid[...]
    out[...] = (x1 + BRANCH * (macc[...] + vec[7:8, :])).astype(bf16)
    hat, scale = norm_parts(x1)
    dh = dacc[...]
    gvec[1:2, :] = jnp.sum(dh * hat, 0, keepdims=True)
    gvec[2:3, :] = jnp.sum(dh, 0, keepdims=True)
    e = dh * vec[5:6, :]
    back = scale * (e - jnp.mean(e, -1, keepdims=True) - hat * jnp.mean(e * hat, -1, keepdims=True))
    dx = cot[...].astype(f32) + back
    dx1[...] = dx
    dlow = (BRANCH * dx).astype(bf16)
    da[...] = dlow
    gvec[0:1, :] = jnp.sum(dlow.astype(f32), 0, keepdims=True)
    for k, o in enumerate((d0, d1, d2, d3)):
        o[...] = dg(dlow, wo[k], NN).astype(bf16)


def grad_fc_kernel(
    place, du, h2, da, a0, a1, a2, a3, s0, s1, k0, k1, wide, narrow,
):
    b, s = place[0], place[1]
    outs = ((k0, k1), (s0, s1))
    for m in range(FB):
        z = (b // 2) ^ (m // 2)
        wide[...] = dg(h2[...], du[b ^ m], TN).astype(bf16)
        for k in range(PARTS):
            outs[k % 2][k // 2][m % 2, z, 0:ROWS, :] = wide[
                pl.ds(pl.multiple_of((s ^ k) * ROWS, 16), ROWS), :
            ]
    for k, a in enumerate((a0, a1, a2, a3)):
        narrow[...] = dg(da[...], a[...], TN).astype(bf16)
        for m in range(FB):
            z = (b // 2) ^ (m // 2)
            for i in range(2):
                outs[k % 2][k // 2][m % 2, z, ROWS:, i * GROUP : (i + 1) * GROUP] = narrow[
                    pl.ds(pl.multiple_of((b ^ m) * DB + i * HALF, 16), HALF), :
                ]


def grad_proj_kernel(place, act, dm, send0, send1, keep0, keep1, wide):
    b, s = place[0], place[1]
    for k in range(PARTS):
        outs = (send0, send1) if k % 2 else (keep0, keep1)
        for j in range(2):
            wide[...] = dg(dm[...], act[2 * (s ^ k) + j], TN).astype(bf16)
            for m in range(FB):
                outs[m % 2][(b // 2) ^ (m // 2), k // 2, j * DB : (j + 1) * DB, :] = wide[
                    pl.ds(pl.multiple_of((b ^ m) * DB, 16), DB), :
                ]


def arrange_kernel(place, g0, g1, g2, g3, send, keep, whole):
    b, s = place[0], place[1]
    tail = jnp.zeros((2 * FB, ROWS), f32)
    for k, g in enumerate((g0, g1, g2, g3)):
        for p in range(3):
            at = pl.multiple_of(p * D + (s ^ k) * GROUP, 16)
            whole[pl.ds(at, GROUP), :] = g[p * GROUP : (p + 1) * GROUP, 0:ROWS]
        tail = tail + g[3 * GROUP :, 0:ROWS].astype(f32)
    for m in range(FB):
        out = send if m % 2 else keep
        for i in range(2):
            half = slice(i * ROWS, (i + 1) * ROWS)
            out[m // 2, 0:QH, half] = whole[
                pl.ds(pl.multiple_of((b ^ m) * QB + i * QH, 16), QH), :
            ]
            row = tail[2 * m + i : 2 * m + i + 1, :]
            extra = jnp.concatenate([row, jnp.zeros((7, ROWS), f32)], 0)
            out[m // 2, QH:, half] = extra.astype(bf16)


def adam_refs(refs, outs, grad, rate, decay):
    for out, value in zip(outs, adam_update(*(r[...] for r in refs), grad, rate, decay)):
        out[...] = value


def adam_q_kernel(place, p0, p1, p2, p3, *refs):
    total = (p0[...].astype(f32) + p1[...].astype(f32)) + (
        p2[...].astype(f32) + p3[...].astype(f32)
    )
    grad = jnp.concatenate([total[0:QH, 0:ROWS].T, total[0:QH, ROWS:].T], 1)
    adam_refs(refs[0:3], refs[6:10], grad, D ** (-0.5), matrix_decay)
    row = total[QH : QH + 1, :]
    vec = jnp.concatenate([row[:, i * DB : (i + 1) * DB] for i in range(3)], 0)
    adam_refs(refs[3:6], refs[10:14], vec, 0.5, 0.0)


def adam_a_kernel(place, p0, p1, p2, p3, *refs):
    total = (p0[...].astype(f32) + p1[...].astype(f32)) + (
        p2[...].astype(f32) + p3[...].astype(f32)
    )
    adam_refs(refs[0:3], refs[6:10], total[0:ROWS, :], D ** (-0.5), matrix_decay)
    grad = jnp.concatenate([total[ROWS:, 0:GROUP].T, total[ROWS:, GROUP:].T], 1)
    adam_refs(refs[3:6], refs[10:14], grad, max(1, 16 * D // LEN) ** (-0.5), matrix_decay)


def adam_b_kernel(place, mine, got, *refs):
    total = mine[...] + got[...].astype(f32)
    grad = jnp.concatenate([total[0:DB, :], total[DB:, :]], 1)
    adam_refs(refs[0:3], refs[3:7], grad, FF ** (-0.5), matrix_decay)


def last_kernel(place, dx1, own, other, x, vec, out):
    hat, scale = norm_parts(x[...].astype(f32))
    e = (own[...].astype(f32) + other[...].astype(f32)) * vec[0:1, :]
    back = scale * (e - jnp.mean(e, -1, keepdims=True) - hat * jnp.mean(e * hat, -1, keepdims=True))
    out[...] = (dx1[...] + back).astype(bf16)


def local(
    inputs, cotangent,
    qkv_weight, qkv_first, qkv_second,
    out_weight, out_first, out_second,
    fc_weight, fc_first, fc_second,
    proj_weight, proj_first, proj_second,
    vectors, vector_first, vector_second,
):
    dp = lax.axis_size("dp")
    by_pairs = dp == FB
    b = lax.axis_index("dp").astype(jnp.int32)
    s = lax.axis_index("seq").astype(jnp.int32)
    place = jnp.stack([b if by_pairs else jnp.zeros_like(b), s])
    split = dp // FB

    x = [inputs.reshape(TOK, D)]
    cot = cotangent.reshape(TOK, D)
    x.append(swap(x[0], "seq", 1))
    x.append(swap(x[0], "seq", 2))

    low_qkv = qkv_weight.astype(bf16).T
    low_vec = vectors.astype(bf16)
    low_fc = fc_weight.astype(bf16)
    low_proj = proj_weight.astype(bf16).T
    low_out = out_weight.astype(bf16).T

    def call(kernel, args, outs, scratch, cost, name, spare=4, deps=()):
        return list(vmem_call(kernel, [place, *args], outs, scratch, cost, name, spare, deps))

    def with_vec(weight, value):
        n = weight.shape[0]
        weight = jnp.concatenate([weight[:, :QH], weight[:, QH:]], 2)
        row = jnp.pad(value.reshape(n, 1, 3 * DB), ((0, 0), (0, 7), (0, DB)))
        return jnp.concatenate([weight, row], 1)

    def as_late(fc, proj, out):
        n = fc.shape[0]
        out = out.reshape(n, 2, HALF, ROWS).transpose(0, 2, 1, 3).reshape(n, HALF, FC)
        proj = proj.reshape(n, DB, 2, FC).transpose(0, 2, 1, 3).reshape(n, ROWS, FC)
        return jnp.concatenate([fc, out], 1), proj

    def pairs_first(value):
        return value.reshape((4, 2) + value.shape[1:]).swapaxes(0, 1)

    if by_pairs:
        mine = with_vec(low_qkv[None], low_vec[None])[0]
        late = jnp.concatenate(as_late(low_fc[None], low_proj[None], low_out[None]), 1)[0]
        z_qkv = call(
            stack_kernel, direct([mine] * 4), [shape((4, QP, 2 * ROWS), bf16)], [], 1, "stack_qkv"
        )[0]
        z_qkv, x[2] = tie(z_qkv, x[2])
        x.append(swap(x[2], "seq", 1))
        x_qkv = swap(z_qkv, "dp", 1)
        late, z_qkv = tie(late, z_qkv)
        late = z_exchange(jnp.broadcast_to(late, (4,) + late.shape))
    else:
        x.append(swap(x[2], "seq", 1))
        all_qkv = lax.all_gather(low_qkv, "dp").reshape(FB, QB, ROWS)
        all_vec = lax.all_gather(low_vec, "dp").transpose(1, 0, 2).reshape(3, FB, DB)
        z_qkv, x_qkv = pairs_first(with_vec(all_qkv, all_vec.transpose(1, 0, 2)))
        all_fc = lax.all_gather(low_fc, "dp").reshape(FB, split, ROWS, FC // split)
        all_fc = all_fc.transpose(0, 2, 1, 3).reshape(FB, ROWS, FC)
        all_proj = lax.all_gather(low_proj, "dp").reshape(FB, DB, D)
        all_out = lax.all_gather(low_out, "dp").reshape(FB, DB, ROWS)
        all_a, all_b = as_late(all_fc, all_proj, all_out)
        late_parts = []
        for part in (all_a, all_b):
            own = pairs_first(part)
            other = swap(own, "seq", 2)
            late_parts.append([own[0], own[1], other[0], other[1]])

    x_qkv, x[1], x[3] = tie(x_qkv, x[1], x[3])
    group_shape = shape((3 * GROUP + 2 * FB, ROWS), bf16)
    picked = call(
        pick_kernel, [z_qkv, x_qkv], [group_shape] * PARTS, [pltpu.VMEM((3 * D, ROWS), bf16)],
        2, "pick",
    )
    wq = seq_exchange(picked)
    if by_pairs:
        line = call(
            place_kernel, [late], [shape((4, AR, FC), bf16), shape((4, ROWS, FC), bf16)],
            [], 1, "line", deps=wq[1:],
        )
        x_b, x_a = swap(line[1], "dp", 1), swap(line[0], "dp", 1)
        y_b, y_a = swap(line[1], "seq", 2), swap(line[0], "seq", 2)
        first_deps = [line[0]]
    else:
        first_deps = []

    lse_shape = shape((1, LEN), f32)
    head_shape = shape((LEN, HEAD_DIM), bf16)
    head_space = [pltpu.VMEM((LEN, HEAD_DIM), bf16)]
    qkv0, qkv1, qkv2, wt, head0, lse0, vec, fbias = call(
        first_kernel, [*x, *wq],
        [shape((3, LEN, HEAD_DIM), bf16)] * OWN_HEADS
        + [shape((3 * GROUP, D), bf16), head_shape, lse_shape]
        + [shape((12, D), f32), shape((FB, 1, FC), f32)],
        [pltpu.VMEM((PARTS, 3 * GROUP, ROWS), bf16), pltpu.VMEM((PARTS, FB, 3, DB), f32)], 16, "first", 14,
        deps=first_deps,
    )
    head1, lse1 = call(second_kernel, [qkv1], [head_shape, lse_shape], [], 2, "second", 14)
    if by_pairs:
        x_b, head1 = tie(x_b, head1)
        late_b = [line[1], x_b, y_b, swap(x_b, "seq", 2)]
    *at, lse2 = call(
        third_kernel, [qkv2, head0, head1], [shape((TOK, GROUP), bf16)] * PARTS + [lse_shape],
        head_space, 7, "third", 14,
    )
    if by_pairs:
        y_a, lse2 = tie(y_a, lse2)
        late_parts = [[line[0], x_a, y_a, swap(y_a, "dp", 1)], late_b]
    rows = seq_exchange(at)
    late_parts, rows[1:] = tie(late_parts, rows[1:])
    late_a, late_b = ([w for p in part for w in (p, swap(p, "seq", 1))] for part in late_parts)
    heads = ((qkv0, lse0), (qkv1, lse1), (qkv2, lse2))

    mid_shape = shape((TOK, D), f32)
    wide_shape = shape((FB, TOK, FC), bf16)
    out, act, du, h2, dm, da, dx1, d0, d1, d2, d3, gvec, gfb = call(
        middle_kernel, [*rows, x[0], cot, *late_a, *late_b, vec, fbias],
        [shape((TOK, D), bf16), wide_shape, wide_shape]
        + [shape((TOK, D), bf16)] * 3 + [mid_shape] + [shape((TOK, GROUP), bf16)] * PARTS
        + [shape((4, D), f32), shape((FB, 1, FC), f32)],
        [pltpu.VMEM((PARTS, D, GROUP), bf16), pltpu.VMEM((D, FC), bf16), pltpu.VMEM((D, FC), bf16),
         pltpu.VMEM((TOK, D), f32), pltpu.VMEM((TOK, D), f32), pltpu.VMEM((TOK, D), f32)],
        28, "middle", 10,
    )
    gout = seq_exchange([d0, d1, d2, d3])

    def fold(keep, got, name, deps=()):
        flat = [v.reshape((-1,) + v.shape[-2:]) for v in (*keep, *got)]
        outs = call(
            fold_kernel, flat, [shape(f.shape, bf16) for f in flat[: len(keep)]], [], 0.2, name, 4,
            deps,
        )
        return [o.reshape(k.shape) for o, k in zip(outs, keep)]


    *a_send, a0, a1 = call(
        grad_fc_kernel, [du, h2, da, *rows], [shape((2, 4, AR, FC), bf16)] * 4,
        [pltpu.VMEM((D, FC), bf16), pltpu.VMEM((D, GROUP), bf16)], 0.3, "grad_fc",
    )
    a_got = [swap(p, "seq", 1) for p in a_send]
    *b_send, b0, b1 = call(
        grad_proj_kernel, [act, dm],
        [shape((4, 2, ROWS, FC), bf16)] * 4, [pltpu.VMEM((D, FC), bf16)], 0.3, "grad_proj",
        deps=[a0],
    )
    b_got = [swap(p, "seq", 1) for p in b_send]

    def backward(h, cost, deps):
        qkv, lse = heads[h]
        return call(
            functools.partial(backward_kernel, head=h),
            [qkv, *gout, *at, lse], [shape((3, LEN, HEAD_DIM), bf16)],
            [pltpu.VMEM((LEN, HEAD_DIM), bf16), pltpu.VMEM((LEN, 1), f32),
             pltpu.VMEM((HEAD_DIM, LEN), f32), pltpu.VMEM((HEAD_DIM, LEN), f32)],
            cost, "backward", 14, deps=deps,
        )[0]

    def plain(mine):
        return lax.psum_scatter(mine, "dp", scatter_dimension=0, tiled=False).astype(f32)

    back0 = backward(0, 36, [b0])
    a_mine, a_other = fold([a0, a1], a_got, "fold_a_core", [back0])
    b_mine, b_other = fold([b0, b1], b_got, "fold_b_core", [a_mine])
    back1 = backward(1, 4, [b_mine])
    back2 = backward(2, 4, [back1])
    dk0, dk1, ds0, ds1, gq0, gq1, gq23 = call(
        gather_kernel, [back0, back1, back2, wt, *x, vec, gvec, gfb],
        [shape((TOK, D), bf16)] * 4
        + [group_shape, group_shape, shape((group_shape.shape[0], 2 * ROWS), bf16)],
        [pltpu.VMEM((3 * GROUP, D), f32), pltpu.VMEM((PARTS, 3 * GROUP, ROWS), bf16),
         pltpu.VMEM((PARTS, 1, 3 * GROUP), f32), pltpu.VMEM((PARTS, FB, 3, DB), f32)],
        1, "gather", 8,
    )
    gq1 = swap(gq1, "seq", 1)
    gq23 = swap(gq23, "seq", 2)
    own, other = fold([dk0, dk1], [swap(ds0, "seq", 1), swap(ds1, "seq", 1)], "fold_dh")
    other = swap(other, "seq", 2)
    if by_pairs:
        b_pieces = call(
            line_kernel, [b_mine, swap(b_other, "dp", 1)], [shape((2, ROWS, FC), bf16)] * 4,
            [], 0.2, "fold_b_x", deps=[own],
        )
        a_mine, a_other = call(
            split_kernel, [a_mine, swap(a_other, "seq", 2)], [shape((4, AR, FC), bf16)] * 2,
            [], 0.2, "fold_a_y", deps=[b_pieces[0]],
        )
        b_got = direct(b_pieces)
        gq23, a_mine = tie(gq23, a_mine)
        q_deps = [a_mine]
    else:
        q_deps = []
    gq = [gq0, gq1, gq23, swap(gq23[:, ROWS:], "seq", 1)]
    q_send, q_keep = call(
        arrange_kernel, gq, [shape((4, QP, 2 * ROWS), bf16)] * 2,
        [pltpu.VMEM((3 * D, ROWS), bf16)], 0.2, "arrange", deps=q_deps,
    )
    if by_pairs:
        proj, proj_send = call(
            four_kernel, b_got, [shape((ROWS, FC), f32), shape((ROWS, FC), bf16)],
            [], 0.2, "sum_b", deps=[q_send],
        )
        a_pieces = call(
            line_kernel, [a_mine, swap(a_other, "dp", 1)], [shape((AR, FC), bf16)] * 4,
            [], 0.2, "fold_a_x", deps=[proj_send],
        )
        q_pieces = call(
            pieces_kernel, [q_keep, swap(q_send, "dp", 1)],
            [shape((QP, 2 * ROWS), bf16)] * 4, [], 0.2, "fold_q_x", deps=[a_pieces[0]],
        )
        q_pieces = direct(q_pieces)
        a_pieces = direct(a_pieces)
        proj_got = swap(proj_send, "seq", 2)
    else:
        def flat(mine):
            return mine.swapaxes(0, 1).reshape((FB,) + mine.shape[2:])

        a_got = swap(a_other, "seq", 2)
        all_a = flat(fold([a_mine], [a_got], "fold_a_y")[0])
        b_mine = [p[:, 0] for p in (b_mine, b_other)], [p[:, 1] for p in (b_mine, b_other)]
        b_got = [swap(p, "seq", 2) for p in b_mine[1]]
        all_b = flat(jnp.stack(fold(b_mine[0], b_got, "fold_b_y")))
        fc = all_a[:, :ROWS].reshape(FB, ROWS, split, FC // split).transpose(0, 2, 1, 3)
        sum_fc = plain(fc.reshape(dp, ROWS, FC // split))
        go = all_a[:, ROWS:].reshape(FB, HALF, 2, ROWS).transpose(0, 2, 1, 3)
        sum_out = plain(go.reshape(dp, D // dp, ROWS)).T
        proj = all_b.reshape(FB, 2, DB, FC).transpose(0, 2, 1, 3)
        sum_proj = plain(proj.reshape(dp, D // dp, D)).T
        all_q = flat(jnp.stack([q_keep, q_send]))
        halves = [all_q[:, :QH, :ROWS], all_q[:, :QH, ROWS:]]
        sum_qkv = plain(jnp.concatenate(halves, 1).reshape(dp, 3 * D // dp, ROWS)).T
        vrows = all_q[:, QH].reshape(FB, 4, DB)[:, :3]
        vrows = vrows.reshape(FB, 3, split, DB // split).transpose(0, 2, 1, 3)
        sum_vec = plain(vrows.reshape(dp, 3, DB // split))
    (input_grad,) = call(
        last_kernel, [dx1, own, other, x[0], vec], [shape((TOK, D), bf16)], [], 0.3, "last"
    )

    qkv_set = (qkv_weight, qkv_first, qkv_second)
    out_set = (out_weight, out_first, out_second)
    fc_set = (fc_weight, fc_first, fc_second)
    proj_set = (proj_weight, proj_first, proj_second)
    vec_set = (vectors, vector_first, vector_second)
    if by_pairs:

        def news(group):
            return [shape(group[0].shape, d) for d in (f32, f32, f32, bf16)]

        def turned(group):
            return [v.T for v in group]

        proj_set = turned(proj_set)

        proj_new = call(
            adam_b_kernel, [proj, proj_got, *proj_set], news(proj_set), [], 0.3, "adam_proj"
        )
        proj_new = turned(proj_new)
        new = call(
            adam_a_kernel, [*a_pieces, *fc_set, *out_set], news(fc_set) + news(out_set),
            [], 0.3, "adam_fc", deps=[input_grad, proj_new[0].T],
        )
        fc_new, out_new = new[:4], new[4:]
        new = call(
            adam_q_kernel, [*q_pieces, *qkv_set, *vec_set], news(qkv_set) + news(vec_set),
            [], 0.3, "adam_qkv", deps=[fc_new[0]],
        )
        qkv_new, vec_new = new[:4], new[4:]
    else:
        qkv_new = adam_update(*qkv_set, sum_qkv, D ** (-0.5), matrix_decay)
        out_new = adam_update(*out_set, sum_out, max(1, 16 * D // LEN) ** (-0.5), matrix_decay)
        fc_new = adam_update(*fc_set, sum_fc, D ** (-0.5), matrix_decay)
        proj_new = adam_update(*proj_set, sum_proj, FF ** (-0.5), matrix_decay)
        vec_new = adam_update(*vec_set, sum_vec, 0.5, 0.0)
    return (
        out.reshape(inputs.shape),
        input_grad.reshape(inputs.shape),
        *qkv_new,
        *out_new,
        *fc_new,
        *proj_new,
        *vec_new,
    )


def solution(mesh):
    rows = P("dp", "seq", None)
    block = P("seq", "dp")
    return jax.shard_map(
        local,
        mesh=mesh,
        in_specs=(rows, rows) + (block,) * 15,
        out_specs=(rows, rows) + (block,) * 20,
        check_vma=False,
    )
```

```python
import functools

import jax
import jax.numpy as jnp
from jax import lax
from jax.experimental import pallas as pl
from jax.experimental.pallas import tpu as pltpu
from jax.sharding import PartitionSpec as P

D = 768
HEADS = 12
HEAD_DIM = 64
FF = 3072
DEPTH = 12
LEN = 2048
STEP = 10
PARTS = 4
TOK = LEN // PARTS
OWN_HEADS = HEADS // PARTS
GROUP = OWN_HEADS * HEAD_DIM
ROWS = D // PARTS
FB = 8
FC = FF // FB
DB = D // FB
QB = 3 * D // FB
QH = QB // 2
QP = QH + 8
HALF = DB // 2
AR = ROWS + HALF
LR = AR + ROWS
BRANCH = DEPTH ** (-0.5)
EPS = 1e-05

beta_one = 0.5
beta_two = 0.5
matrix_decay = 0.1

f32 = jnp.float32
bf16 = jnp.bfloat16

NN = (((1,), (0,)), ((), ()))
NT = (((1,), (1,)), ((), ()))
TN = (((0,), (0,)), ((), ()))


def dg(left, right, dims):
    return lax.dot_general(left, right, dims, preferred_element_type=f32)


def adam_update(master, first, second, grad, rate, decay):
    first_new = beta_one * first + (1.0 - beta_one) * grad
    second_new = beta_two * second + (1.0 - beta_two) * grad * grad
    fix_one = 1.0 - beta_one**STEP
    fix_two = 1.0 - beta_two**STEP
    direction = first_new / fix_one / (jnp.sqrt(second_new / fix_two) + 1e-08)
    updated = master - rate * (direction + decay * master)
    return (first_new, second_new, updated, updated.astype(bf16))


def swap(value, axis, k):
    n = lax.axis_size(axis)
    return lax.ppermute(value, axis, [(i, i ^ k) for i in range(n)])


def direct(pieces):
    return [pieces[0]] + [swap(pieces[k], "dp", 2 * k) for k in (1, 2, 3)]


def seq_exchange(values):
    return [values[0]] + [swap(values[k], "seq", k) for k in range(1, PARTS)]


def z_exchange(value):
    groups = [[2 * z + x for z in range(4)] for x in range(2)]
    return lax.all_to_all(value, "dp", 0, 0, axis_index_groups=groups, tiled=True)


def tie(*values):
    return lax.optimization_barrier(values)


VM = pl.BlockSpec(memory_space=pltpu.VMEM)
SM = pl.BlockSpec(memory_space=pltpu.SMEM)


def space(item):
    dims = list(item.shape)
    dims[-1] = -(-dims[-1] // 128) * 128
    if len(dims) > 1:
        dims[-2] = -(-dims[-2] // 8) * 8
    size = jnp.dtype(item.dtype).itemsize
    for d in dims:
        size *= d
    return size


def vmem_call(kernel, args, outs, scratch, flops, name, spare=4, deps=()):
    n = len(args)

    def body(*refs):
        kernel(*refs[:n], *refs[n + len(deps) :])

    need = sum(space(a) for a in (*args[1:], *outs, *scratch)) + spare * 2**20
    return pl.pallas_call(
        body,
        out_shape=tuple(outs),
        in_specs=[SM] + [VM] * (n - 1) + [pl.BlockSpec(memory_space=pl.ANY)] * len(deps),
        out_specs=tuple([VM] * len(outs)),
        scratch_shapes=list(scratch),
        compiler_params=pltpu.CompilerParams(vmem_limit_bytes=need),
        cost_estimate=pl.CostEstimate(
            flops=int(flops * 0.5e9), bytes_accessed=1024, transcendentals=0
        ),
        name=name,
    )(*args, *deps)


def shape(dims, dtype):
    return jax.ShapeDtypeStruct(dims, dtype)


def norm_parts(values):
    centre = values - jnp.mean(values, -1, keepdims=True)
    spread = jnp.mean(centre * centre, -1, keepdims=True)
    scale = lax.rsqrt(spread + EPS)
    return centre * scale, scale


def stack_kernel(place, p0, p1, p2, p3, out):
    for k, p in enumerate((p0, p1, p2, p3)):
        out[k] = p[...]


def place_kernel(place, p, a, b):
    for k in range(4):
        a[k] = p[k, 0:AR, :]
        b[k] = p[k, AR:, :]


def pick_kernel(place, z, x, o0, o1, o2, o3, whole):
    b, s = place[0], place[1]
    for m in range(FB):
        part = (z, x)[m % 2]
        for i in range(2):
            whole[pl.ds(pl.multiple_of((b ^ m) * QB + i * QH, 16), QH), :] = part[
                m // 2, 0:QH, i * ROWS : (i + 1) * ROWS
            ]
    tail = jnp.concatenate(
        [
            (z, x)[m % 2][m // 2, QH : QH + 1, i * ROWS : (i + 1) * ROWS]
            for m in range(FB)
            for i in range(2)
        ],
        0,
    )
    for k, out in enumerate((o0, o1, o2, o3)):
        for p in range(3):
            at = pl.multiple_of(p * D + (s ^ k) * GROUP, 16)
            out[p * GROUP : (p + 1) * GROUP, :] = whole[pl.ds(at, GROUP), :]
        out[3 * GROUP :, :] = tail


def fold_kernel(place, *refs):
    n = len(refs) // 3
    for keep, got, out in zip(refs[:n], refs[n : 2 * n], refs[2 * n :]):

        def step(j, _):
            out[j] = (keep[j].astype(f32) + got[j].astype(f32)).astype(bf16)
            return 0

        lax.fori_loop(0, keep.shape[0], step, 0)


def pieces_kernel(place, keep, got, *outs):
    for k, out in enumerate(outs):
        out[...] = (keep[k].astype(f32) + got[k].astype(f32)).astype(bf16)


def split_kernel(place, keep, got, mine, other):
    def step(j, _):
        for i, out in enumerate((mine, other)):
            out[j] = (keep[i, j].astype(f32) + got[i, j].astype(f32)).astype(bf16)
        return 0

    lax.fori_loop(0, keep.shape[1], step, 0)


def line_kernel(place, keep, got, *outs):
    for k, out in enumerate(outs):
        j = (place[0] // 2) ^ k
        out[...] = (keep[j].astype(f32) + got[j].astype(f32)).astype(bf16)


def four_kernel(place, p, mine, other):
    for i, out in enumerate((mine, other)):
        total = (p[0, i].astype(f32) + p[1, i].astype(f32)) + (
            p[2, i].astype(f32) + p[3, i].astype(f32)
        )
        out[...] = total.astype(out.dtype)


def attend(qkv, lse, heads_out):
    for i in range(PARTS):
        qi = qkv[0, i * TOK : (i + 1) * TOK, :]
        n = (i + 1) * TOK
        sc = dg(qkv[1, 0:n, :], qi, NT)
        kp = lax.broadcasted_iota(jnp.int32, (TOK, TOK), 0)
        qp = lax.broadcasted_iota(jnp.int32, (TOK, TOK), 1)
        last = jnp.where(kp <= qp, sc[i * TOK :], -1e30)
        mx = jnp.max(last, 0, keepdims=True)
        if i:
            mx = jnp.maximum(mx, jnp.max(sc[: i * TOK], 0, keepdims=True))
        e_last = jnp.exp(last - mx)
        total = jnp.sum(e_last, 0, keepdims=True)
        e = e_last.astype(bf16)
        if i:
            e_first = jnp.exp(sc[: i * TOK] - mx)
            total = total + jnp.sum(e_first, 0, keepdims=True)
            e = jnp.concatenate([e_first.astype(bf16), e], 0)
        o = dg(qkv[2, 0:n, :], e, TN) / total
        heads_out[i * TOK : (i + 1) * TOK, :] = o.T.astype(bf16)
        lse[:, i * TOK : (i + 1) * TOK] = mx + jnp.log(total)


def first_kernel(
    place, x0, x1, x2, x3, w0, w1, w2, w3,
    qkv0, qkv1, qkv2, wt, heads_out, lse, vec, fbias, pieces, blocks,
):
    b, s = place[0], place[1]
    for k, w in enumerate((w0, w1, w2, w3)):
        pieces[s ^ k] = w[0 : 3 * GROUP, :]
        tail = w[3 * GROUP :, :].astype(f32)
        for m in range(FB):
            blocks[s ^ k, b ^ m, 0:1, :] = tail[2 * m : 2 * m + 1, 0:DB]
            blocks[s ^ k, b ^ m, 1:2, :] = tail[2 * m : 2 * m + 1, DB : 2 * DB]
            blocks[s ^ k, b ^ m, 2:3, :] = tail[2 * m + 1 : 2 * m + 2, 0:DB]
    for j in range(PARTS):
        wt[:, j * ROWS : (j + 1) * ROWS] = pieces[j]
    qbias = jnp.zeros((1, GROUP), f32)
    vbias = jnp.zeros((1, GROUP), f32)
    for r in range(12):
        row = jnp.concatenate([blocks[r // 3, m, r % 3 : r % 3 + 1, :] for m in range(FB)], 1)
        vec[r : r + 1, :] = row
        for m in range(PARTS):
            mine = row[:, m * GROUP : (m + 1) * GROUP]
            if r == 2:
                qbias = jnp.where(s == m, mine, qbias)
            if r == 3:
                vbias = jnp.where(s == m, mine, vbias)
        for m in range(2):
            if r >= 8:
                fbias[2 * (r - 8) + m] = row[:, m * FC : (m + 1) * FC]
    bias = jnp.concatenate([qbias, jnp.zeros((1, GROUP), f32), vbias], 1)
    for k, x in enumerate((x0, x1, x2, x3)):
        rows = pl.ds(pl.multiple_of((s ^ k) * TOK, TOK), TOK)
        hat, _ = norm_parts(x[...].astype(f32))
        h = (hat * vec[0:1, :] + vec[1:2, :]).astype(bf16)
        r = (dg(h, wt[...], NT) + bias).astype(bf16)
        for i in range(3 * OWN_HEADS):
            part = r[:, i * HEAD_DIM : (i + 1) * HEAD_DIM]
            if i < OWN_HEADS:
                part = (part.astype(f32) * HEAD_DIM ** (-0.5)).astype(bf16)
            (qkv0, qkv1, qkv2)[i % OWN_HEADS][i // OWN_HEADS, rows, :] = part
    attend(qkv0, lse, heads_out)


def second_kernel(place, qkv, heads_out, lse):
    attend(qkv, lse, heads_out)


def third_kernel(place, qkv, head0, head1, at0, at1, at2, at3, lse, head2):
    s = place[1]
    attend(qkv, lse, head2)
    for k, at in enumerate((at0, at1, at2, at3)):
        rows = pl.ds(pl.multiple_of((s ^ k) * TOK, TOK), TOK)
        for i, head in enumerate((head0, head1, head2)):
            at[:, i * HEAD_DIM : (i + 1) * HEAD_DIM] = head[rows, :]


def backward_kernel(
    place, qkv, g0, g1, g2, g3, at0, at1, at2, at3, lse,
    dheads, gout, delta, dkt, dvt, *, head,
):
    s = place[1]
    lanes = slice(head * HEAD_DIM, (head + 1) * HEAD_DIM)
    for k, (g, at) in enumerate(zip((g0, g1, g2, g3), (at0, at1, at2, at3))):
        rows = pl.ds(pl.multiple_of((s ^ k) * TOK, TOK), TOK)
        gv = g[:, lanes]
        gout[rows, :] = gv
        delta[rows, :] = jnp.sum(gv.astype(f32) * at[:, lanes].astype(f32), 1, keepdims=True)
    for i in range(PARTS):
        cut = slice(i * TOK, (i + 1) * TOK)
        qi = qkv[0, cut, :]
        gi = gout[cut, :]
        di = delta[cut, :]
        li = lse[:, cut].T
        dq = jnp.zeros((TOK, HEAD_DIM), f32)
        for j in range(i + 1):
            keys = slice(j * TOK, (j + 1) * TOK)
            kj = qkv[1, keys, :]
            vj = qkv[2, keys, :]
            sc = dg(qi, kj, NT)
            if j == i:
                qp = lax.broadcasted_iota(jnp.int32, (TOK, TOK), 0)
                kp = lax.broadcasted_iota(jnp.int32, (TOK, TOK), 1)
                sc = jnp.where(kp <= qp, sc, -1e30)
            p = jnp.exp(sc - li)
            dp = dg(gi, vj, NT)
            ds = (p * (dp - di)).astype(bf16)
            dq = dq + dg(ds, kj, NN)
            dv = dg(gi, p.astype(bf16), TN)
            dk = dg(qi, ds, TN)
            if j == i:
                dkt[:, keys] = dk
                dvt[:, keys] = dv
            else:
                dkt[:, keys] += dk
                dvt[:, keys] += dv
        dheads[0, cut, :] = (dq * HEAD_DIM ** (-0.5)).astype(bf16)
    for j in range(PARTS):
        keys = slice(j * TOK, (j + 1) * TOK)
        dheads[1, keys, :] = dkt[:, keys].T.astype(bf16)
        dheads[2, keys, :] = dvt[:, keys].T.astype(bf16)


def gather_kernel(
    place, e0, e1, e2, wt, x0, x1, x2, x3, vec, gvec, gfb,
    dk0, dk1, ds0, ds1, gq0, gq1, gq23, gsum, gpieces, gbias, rows_of,
):
    b, s = place[0], place[1]
    gsum[...] = jnp.zeros_like(gsum)
    sums = jnp.zeros((1, 3 * GROUP), f32)
    gain = jnp.zeros((1, D), f32)
    shift = jnp.zeros((1, D), f32)
    for k, x in enumerate((x0, x1, x2, x3)):
        rows = pl.ds(pl.multiple_of((s ^ k) * TOK, TOK), TOK)
        dqkv = jnp.concatenate([e[i, rows, :] for i in range(3) for e in (e0, e1, e2)], 1)
        hat, _ = norm_parts(x[...].astype(f32))
        h = (hat * vec[0:1, :] + vec[1:2, :]).astype(bf16)
        gsum[...] += dg(dqkv, h, TN)
        sums = sums + jnp.sum(dqkv.astype(f32), 0, keepdims=True)
        part = dg(dqkv, wt[...], NN)
        (dk0, ds0, dk1, ds1)[k][...] = part.astype(bf16)
        gain = gain + jnp.sum(part * hat, 0, keepdims=True)
        shift = shift + jnp.sum(part, 0, keepdims=True)
    for m in range(PARTS):
        gpieces[m] = gsum[:, m * ROWS : (m + 1) * ROWS].astype(bf16)
    outs = (
        (gq0, slice(0, ROWS)),
        (gq1, slice(0, ROWS)),
        (gq23, slice(0, ROWS)),
        (gq23, slice(ROWS, 2 * ROWS)),
    )
    for k, (out, lanes) in enumerate(outs):
        out[0 : 3 * GROUP, lanes] = gpieces[s ^ k]
    gbias[...] = jnp.zeros_like(gbias)
    gbias[s] = sums
    qrow = jnp.concatenate([gbias[m, :, 0:GROUP] for m in range(PARTS)], 1)
    vrow = jnp.concatenate([gbias[m, :, 2 * GROUP : 3 * GROUP] for m in range(PARTS)], 1)
    for r in range(12):
        if r < 4:
            row = (gain, shift, qrow, vrow)[r]
        elif r < 8:
            row = gvec[r - 4 : r - 3, :]
        else:
            row = jnp.concatenate([gfb[2 * (r - 8)], gfb[2 * (r - 8) + 1]], 1)
        for m in range(FB):
            rows_of[r // 3, m, r % 3 : r % 3 + 1, :] = row[:, m * DB : (m + 1) * DB]
    for k, (out, lanes) in enumerate(outs):
        tail = []
        for m in range(FB):
            part = rows_of[s ^ k, b ^ m]
            tail.append(jnp.concatenate([part[0:1, :], part[1:2, :]], 1))
            tail.append(jnp.concatenate([part[2:3, :], jnp.zeros((1, DB), f32)], 1))
        out[3 * GROUP :, lanes] = jnp.concatenate(tail, 0).astype(bf16)


def middle_kernel(
    place, a0, a1, a2, a3, x, cot, l0, l1, l2, l3, l4, l5, l6, l7,
    p0, p1, p2, p3, p4, p5, p6, p7, vec, fbias,
    out, act, du, h2, dm, da, dx1, d0, d1, d2, d3, gvec, gfb, wo, wf, wp, mid, macc, dacc,
):
    b, s = place[0], place[1]
    weights = (l0, l1, l2, l3, l4, l5, l6, l7)
    downs = (p0, p1, p2, p3, p4, p5, p6, p7)
    for k in range(PARTS):
        for m in range(FB):
            low = weights[4 * (k // 2) + 2 * (m % 2) + k % 2]
            for i in range(2):
                wo[k, pl.ds(pl.multiple_of((b ^ m) * DB + i * HALF, 16), HALF), :] = low[
                    (b // 2) ^ (m // 2), ROWS:AR, i * GROUP : (i + 1) * GROUP
                ]
    proj = dg(a0[...], wo[0], NT)
    for k, a in ((1, a1), (2, a2), (3, a3)):
        proj = proj + dg(a[...], wo[k], NT)
    x1 = x[...].astype(f32) + BRANCH * (proj + vec[4:5, :])
    mid[...] = x1
    hat, _ = norm_parts(x1)
    h2[...] = (hat * vec[5:6, :] + vec[6:7, :]).astype(bf16)
    low = (BRANCH * cot[...].astype(f32)).astype(bf16)
    dm[...] = low
    gvec[3:4, :] = jnp.sum(low.astype(f32), 0, keepdims=True)
    macc[...] = jnp.zeros_like(macc)
    dacc[...] = jnp.zeros_like(dacc)

    def chunk(z, _, q):
        j = (b % 2) ^ q
        f = 2 * z + j
        for m in range(PARTS):
            part = weights[4 * (m // 2) + 2 * q + m % 2]
            wf[pl.ds(pl.multiple_of((s ^ m) * ROWS, 16), ROWS), :] = part[z, 0:ROWS, :]
        for k in range(PARTS):

            @pl.when((s ^ z) == k)
            def _():
                for m in range(FB):
                    part = downs[4 * (k // 2) + 2 * (m % 2) + k % 2]
                    wp[pl.ds(pl.multiple_of((b ^ m) * DB, 16), DB), :] = part[
                        (b // 2) ^ (m // 2), pl.ds(pl.multiple_of(j * DB, 16), DB), :
                    ]

        u = dg(h2[...], wf[...], NN) + fbias[f]
        coef = (2.0 / jnp.pi) ** 0.5
        th = jnp.tanh(coef * (u + 0.044715 * (u * u * u)))
        half = 0.5 * (1.0 + th)
        av = (u * half).astype(bf16)
        act[f] = av
        slope = half + 0.5 * u * (1.0 - th * th) * (coef * (1.0 + 3 * 0.044715 * (u * u)))
        dv = (dg(dm[...], wp[...], NN) * slope).astype(bf16)
        du[f] = dv
        gfb[f] = jnp.sum(dv.astype(f32), 0, keepdims=True)
        macc[...] += dg(av, wp[...], NT)
        dacc[...] += dg(dv, wf[...], NT)
        return 0

    for q in range(2):
        lax.fori_loop(0, 4, functools.partial(chunk, q=q), 0)
    x1 = mid[...]
    out[...] = (x1 + BRANCH * (macc[...] + vec[7:8, :])).astype(bf16)
    hat, scale = norm_parts(x1)
    dh = dacc[...]
    gvec[1:2, :] = jnp.sum(dh * hat, 0, keepdims=True)
    gvec[2:3, :] = jnp.sum(dh, 0, keepdims=True)
    e = dh * vec[5:6, :]
    back = scale * (e - jnp.mean(e, -1, keepdims=True) - hat * jnp.mean(e * hat, -1, keepdims=True))
    dx = cot[...].astype(f32) + back
    dx1[...] = dx
    dlow = (BRANCH * dx).astype(bf16)
    da[...] = dlow
    gvec[0:1, :] = jnp.sum(dlow.astype(f32), 0, keepdims=True)
    for k, o in enumerate((d0, d1, d2, d3)):
        o[...] = dg(dlow, wo[k], NN).astype(bf16)


def grad_fc_kernel(
    place, du, h2, da, a0, a1, a2, a3, s0, s1, k0, k1, wide, narrow,
):
    b, s = place[0], place[1]
    outs = ((k0, k1), (s0, s1))
    for m in range(FB):
        z = (b // 2) ^ (m // 2)
        wide[...] = dg(h2[...], du[b ^ m], TN).astype(bf16)
        for k in range(PARTS):
            outs[k % 2][k // 2][m % 2, z, 0:ROWS, :] = wide[
                pl.ds(pl.multiple_of((s ^ k) * ROWS, 16), ROWS), :
            ]
    for k, a in enumerate((a0, a1, a2, a3)):
        narrow[...] = dg(da[...], a[...], TN).astype(bf16)
        for m in range(FB):
            z = (b // 2) ^ (m // 2)
            for i in range(2):
                outs[k % 2][k // 2][m % 2, z, ROWS:, i * GROUP : (i + 1) * GROUP] = narrow[
                    pl.ds(pl.multiple_of((b ^ m) * DB + i * HALF, 16), HALF), :
                ]


def grad_proj_kernel(place, act, dm, send0, send1, keep0, keep1, wide):
    b, s = place[0], place[1]
    for k in range(PARTS):
        outs = (send0, send1) if k % 2 else (keep0, keep1)
        for j in range(2):
            wide[...] = dg(dm[...], act[2 * (s ^ k) + j], TN).astype(bf16)
            for m in range(FB):
                outs[m % 2][(b // 2) ^ (m // 2), k // 2, j * DB : (j + 1) * DB, :] = wide[
                    pl.ds(pl.multiple_of((b ^ m) * DB, 16), DB), :
                ]


def arrange_kernel(place, g0, g1, g2, g3, send, keep, whole):
    b, s = place[0], place[1]
    tail = jnp.zeros((2 * FB, ROWS), f32)
    lanes = slice(0, ROWS)
    for k, g in enumerate((g0, g1, g2, g3)):
        for p in range(3):
            at = pl.multiple_of(p * D + (s ^ k) * GROUP, 16)
            whole[pl.ds(at, GROUP), :] = g[p * GROUP : (p + 1) * GROUP, lanes]
        tail = tail + g[3 * GROUP :, lanes].astype(f32)
    for m in range(FB):
        out = send if m % 2 else keep
        for i in range(2):
            half = slice(i * ROWS, (i + 1) * ROWS)
            out[m // 2, 0:QH, half] = whole[
                pl.ds(pl.multiple_of((b ^ m) * QB + i * QH, 16), QH), :
            ]
            row = tail[2 * m + i : 2 * m + i + 1, :]
            extra = jnp.concatenate([row, jnp.zeros((7, ROWS), f32)], 0)
            out[m // 2, QH:, half] = extra.astype(bf16)


def adam_refs(refs, outs, grad, rate, decay):
    for out, value in zip(outs, adam_update(*(r[...] for r in refs), grad, rate, decay)):
        out[...] = value


def adam_q_kernel(place, p0, p1, p2, p3, *refs):
    total = (p0[...].astype(f32) + p1[...].astype(f32)) + (
        p2[...].astype(f32) + p3[...].astype(f32)
    )
    grad = jnp.concatenate([total[0:QH, 0:ROWS].T, total[0:QH, ROWS:].T], 1)
    adam_refs(refs[0:3], refs[6:10], grad, D ** (-0.5), matrix_decay)
    row = total[QH : QH + 1, :]
    vec = jnp.concatenate([row[:, i * DB : (i + 1) * DB] for i in range(3)], 0)
    adam_refs(refs[3:6], refs[10:14], vec, 0.5, 0.0)


def adam_a_kernel(place, p0, p1, p2, p3, *refs):
    total = (p0[...].astype(f32) + p1[...].astype(f32)) + (
        p2[...].astype(f32) + p3[...].astype(f32)
    )
    adam_refs(refs[0:3], refs[6:10], total[0:ROWS, :], D ** (-0.5), matrix_decay)
    grad = jnp.concatenate([total[ROWS:, 0:GROUP].T, total[ROWS:, GROUP:].T], 1)
    adam_refs(refs[3:6], refs[10:14], grad, max(1, 16 * D // LEN) ** (-0.5), matrix_decay)


def adam_b_kernel(place, mine, got, *refs):
    total = mine[...] + got[...].astype(f32)
    grad = jnp.concatenate([total[0:DB, :], total[DB:, :]], 1)
    adam_refs(refs[0:3], refs[3:7], grad, FF ** (-0.5), matrix_decay)


def last_kernel(place, dx1, own, other, x, vec, out):
    hat, scale = norm_parts(x[...].astype(f32))
    e = (own[...].astype(f32) + other[...].astype(f32)) * vec[0:1, :]
    back = scale * (e - jnp.mean(e, -1, keepdims=True) - hat * jnp.mean(e * hat, -1, keepdims=True))
    out[...] = (dx1[...] + back).astype(bf16)


def local(
    inputs, cotangent,
    qkv_weight, qkv_first, qkv_second,
    out_weight, out_first, out_second,
    fc_weight, fc_first, fc_second,
    proj_weight, proj_first, proj_second,
    vectors, vector_first, vector_second,
):
    dp = lax.axis_size("dp")
    by_pairs = dp == FB
    b = lax.axis_index("dp").astype(jnp.int32)
    s = lax.axis_index("seq").astype(jnp.int32)
    place = jnp.stack([b if by_pairs else jnp.zeros_like(b), s])
    split = dp // FB

    x = [inputs.reshape(TOK, D)]
    cot = cotangent.reshape(TOK, D)
    x.append(swap(x[0], "seq", 1))
    x.append(swap(x[0], "seq", 2))

    low_qkv = qkv_weight.astype(bf16).T
    low_vec = vectors.astype(bf16)
    low_fc = fc_weight.astype(bf16)
    low_proj = proj_weight.astype(bf16).T
    low_out = out_weight.astype(bf16).T

    def call(kernel, args, outs, scratch, cost, name, spare=4, deps=()):
        return list(vmem_call(kernel, [place, *args], outs, scratch, cost, name, spare, deps))

    def with_vec(weight, value):
        n = weight.shape[0]
        weight = jnp.concatenate([weight[:, :QH], weight[:, QH:]], 2)
        row = jnp.pad(value.reshape(n, 1, 3 * DB), ((0, 0), (0, 7), (0, DB)))
        return jnp.concatenate([weight, row], 1)

    def as_late(fc, proj, out):
        n = fc.shape[0]
        out = out.reshape(n, 2, HALF, ROWS).transpose(0, 2, 1, 3).reshape(n, HALF, FC)
        proj = proj.reshape(n, DB, 2, FC).transpose(0, 2, 1, 3).reshape(n, ROWS, FC)
        return jnp.concatenate([fc, out], 1), proj

    def pairs_first(value):
        return value.reshape((4, 2) + value.shape[1:]).swapaxes(0, 1)

    if by_pairs:
        mine = with_vec(low_qkv[None], low_vec[None])[0]
        late = jnp.concatenate(as_late(low_fc[None], low_proj[None], low_out[None]), 1)[0]
        z_qkv = call(
            stack_kernel, direct([mine] * 4), [shape((4, QP, 2 * ROWS), bf16)], [], 1, "stack_qkv"
        )[0]
        z_qkv, x[2] = tie(z_qkv, x[2])
        x.append(swap(x[2], "seq", 1))
        x_qkv = swap(z_qkv, "dp", 1)
        late, x[3] = tie(late, x[3])
        late = z_exchange(jnp.broadcast_to(late, (4,) + late.shape))
    else:
        x.append(swap(x[2], "seq", 1))
        all_qkv = lax.all_gather(low_qkv, "dp").reshape(FB, QB, ROWS)
        all_vec = lax.all_gather(low_vec, "dp").transpose(1, 0, 2).reshape(3, FB, DB)
        z_qkv, x_qkv = pairs_first(with_vec(all_qkv, all_vec.transpose(1, 0, 2)))
        all_fc = lax.all_gather(low_fc, "dp").reshape(FB, split, ROWS, FC // split)
        all_fc = all_fc.transpose(0, 2, 1, 3).reshape(FB, ROWS, FC)
        all_proj = lax.all_gather(low_proj, "dp").reshape(FB, DB, D)
        all_out = lax.all_gather(low_out, "dp").reshape(FB, DB, ROWS)
        all_a, all_b = as_late(all_fc, all_proj, all_out)
        late_parts = []
        for part in (all_a, all_b):
            own = pairs_first(part)
            other = swap(own, "seq", 2)
            late_parts.append([own[0], own[1], other[0], other[1]])

    x_qkv, x[1], x[3] = tie(x_qkv, x[1], x[3])
    group_shape = shape((3 * GROUP + 2 * FB, ROWS), bf16)
    picked = call(
        pick_kernel, [z_qkv, x_qkv], [group_shape] * PARTS, [pltpu.VMEM((3 * D, ROWS), bf16)],
        2, "pick",
    )
    wq = seq_exchange(picked)
    if by_pairs:
        line = call(
            place_kernel, [late], [shape((4, AR, FC), bf16), shape((4, ROWS, FC), bf16)],
            [], 1, "line", deps=wq[1:],
        )
        x_b, x_a = swap(line[1], "dp", 1), swap(line[0], "dp", 1)
        y_b, y_a = swap(line[1], "seq", 2), swap(line[0], "seq", 2)
        first_deps = [line[0]]
    else:
        first_deps = []

    lse_shape = shape((1, LEN), f32)
    head_shape = shape((LEN, HEAD_DIM), bf16)
    head_space = [pltpu.VMEM((LEN, HEAD_DIM), bf16)]
    qkv0, qkv1, qkv2, wt, head0, lse0, vec, fbias = call(
        first_kernel, [*x, *wq],
        [shape((3, LEN, HEAD_DIM), bf16)] * OWN_HEADS
        + [shape((3 * GROUP, D), bf16), head_shape, lse_shape]
        + [shape((12, D), f32), shape((FB, 1, FC), f32)],
        [pltpu.VMEM((PARTS, 3 * GROUP, ROWS), bf16), pltpu.VMEM((PARTS, FB, 3, DB), f32)], 16, "first", 14,
        deps=first_deps,
    )
    head1, lse1 = call(second_kernel, [qkv1], [head_shape, lse_shape], [], 2, "second", 14)
    if by_pairs:
        x_b, head1 = tie(x_b, head1)
        late_b = [line[1], x_b, y_b, swap(x_b, "seq", 2)]
    *at, lse2 = call(
        third_kernel, [qkv2, head0, head1], [shape((TOK, GROUP), bf16)] * PARTS + [lse_shape],
        head_space, 7, "third", 14,
    )
    if by_pairs:
        y_a, lse2 = tie(y_a, lse2)
        late_parts = [[line[0], x_a, y_a, swap(y_a, "dp", 1)], late_b]
    rows = seq_exchange(at)
    late_parts, rows[1:] = tie(late_parts, rows[1:])
    late_a, late_b = ([w for p in part for w in (p, swap(p, "seq", 1))] for part in late_parts)
    heads = ((qkv0, lse0), (qkv1, lse1), (qkv2, lse2))

    mid_shape = shape((TOK, D), f32)
    wide_shape = shape((FB, TOK, FC), bf16)
    out, act, du, h2, dm, da, dx1, d0, d1, d2, d3, gvec, gfb = call(
        middle_kernel, [*rows, x[0], cot, *late_a, *late_b, vec, fbias],
        [shape((TOK, D), bf16), wide_shape, wide_shape]
        + [shape((TOK, D), bf16)] * 3 + [mid_shape] + [shape((TOK, GROUP), bf16)] * PARTS
        + [shape((4, D), f32), shape((FB, 1, FC), f32)],
        [pltpu.VMEM((PARTS, D, GROUP), bf16), pltpu.VMEM((D, FC), bf16), pltpu.VMEM((D, FC), bf16),
         pltpu.VMEM((TOK, D), f32), pltpu.VMEM((TOK, D), f32), pltpu.VMEM((TOK, D), f32)],
        28, "middle", 10,
    )
    gout = seq_exchange([d0, d1, d2, d3])

    def fold(keep, got, name, deps=()):
        flat = [v.reshape((-1,) + v.shape[-2:]) for v in (*keep, *got)]
        outs = call(
            fold_kernel, flat, [shape(f.shape, bf16) for f in flat[: len(keep)]], [], 0.2, name, 4,
            deps,
        )
        return [o.reshape(k.shape) for o, k in zip(outs, keep)]


    *a_send, a0, a1 = call(
        grad_fc_kernel, [du, h2, da, *rows], [shape((2, 4, AR, FC), bf16)] * 4,
        [pltpu.VMEM((D, FC), bf16), pltpu.VMEM((D, GROUP), bf16)], 0.3, "grad_fc",
    )
    a_got = [swap(p, "seq", 1) for p in a_send]
    *b_send, b0, b1 = call(
        grad_proj_kernel, [act, dm],
        [shape((4, 2, ROWS, FC), bf16)] * 4, [pltpu.VMEM((D, FC), bf16)], 0.3, "grad_proj",
        deps=[a0],
    )
    b_got = [swap(p, "seq", 1) for p in b_send]

    def backward(h, cost, deps):
        qkv, lse = heads[h]
        return call(
            functools.partial(backward_kernel, head=h),
            [qkv, *gout, *at, lse], [shape((3, LEN, HEAD_DIM), bf16)],
            [pltpu.VMEM((LEN, HEAD_DIM), bf16), pltpu.VMEM((LEN, 1), f32),
             pltpu.VMEM((HEAD_DIM, LEN), f32), pltpu.VMEM((HEAD_DIM, LEN), f32)],
            cost, "backward", 14, deps=deps,
        )[0]

    def plain(mine):
        return lax.psum_scatter(mine, "dp", scatter_dimension=0, tiled=False).astype(f32)

    back0 = backward(0, 36, [b0])
    a_mine, a_other = fold([a0, a1], a_got, "fold_a_core", [back0])
    b_mine, b_other = fold([b0, b1], b_got, "fold_b_core", [a_mine])
    back1 = backward(1, 4, [b_mine])
    back2 = backward(2, 4, [back1])
    dk0, dk1, ds0, ds1, gq0, gq1, gq23 = call(
        gather_kernel, [back0, back1, back2, wt, *x, vec, gvec, gfb],
        [shape((TOK, D), bf16)] * 4
        + [group_shape, group_shape, shape((group_shape.shape[0], 2 * ROWS), bf16)],
        [pltpu.VMEM((3 * GROUP, D), f32), pltpu.VMEM((PARTS, 3 * GROUP, ROWS), bf16),
         pltpu.VMEM((PARTS, 1, 3 * GROUP), f32), pltpu.VMEM((PARTS, FB, 3, DB), f32)],
        1, "gather", 8,
    )
    gq23 = swap(gq23, "seq", 2)
    if by_pairs:
        a_mine, a_other = call(
            split_kernel, [a_mine, swap(a_other, "seq", 2)], [shape((4, AR, FC), bf16)] * 2,
            [], 0.2, "fold_a_y", deps=[dk0],
        )
        (b_mine,) = fold([b_mine], [swap(b_other, "dp", 1)], "fold_b_x", [a_mine])
        dh_deps = [b_mine]
        b_got = z_exchange(b_mine)
    else:
        dh_deps = []
    own, other = fold([dk0, dk1], [swap(ds0, "seq", 1), swap(ds1, "seq", 1)], "fold_dh", dh_deps)
    gq23, gq1, own = tie(gq23, gq1, own)
    gq = [gq0, swap(gq1, "seq", 1), gq23, swap(gq23[:, ROWS:], "seq", 1)]
    q_deps = [own]
    if by_pairs:
        a_pieces = call(
            line_kernel, [a_mine, swap(a_other, "dp", 1)], [shape((AR, FC), bf16)] * 4,
            [], 0.2, "fold_a_x", deps=[own],
        )
        q_deps = [a_pieces[0]]
    q_send, q_keep = call(
        arrange_kernel, gq, [shape((4, QP, 2 * ROWS), bf16)] * 2,
        [pltpu.VMEM((3 * D, ROWS), bf16)], 0.2, "arrange", deps=q_deps,
    )
    other, q_send = tie(other, q_send)
    other = swap(other, "seq", 2)
    if by_pairs:
        proj, proj_send = call(
            four_kernel, [b_got], [shape((ROWS, FC), f32), shape((ROWS, FC), bf16)],
            [], 0.2, "sum_b", deps=[q_send],
        )
        q_pieces = call(
            pieces_kernel, [q_keep, swap(q_send, "dp", 1)],
            [shape((QP, 2 * ROWS), bf16)] * 4, [], 0.2, "fold_q_x", deps=[proj_send],
        )
        q_pieces = direct(q_pieces)
        a_pieces = direct(a_pieces)
        proj_got = swap(proj_send, "seq", 2)
    else:
        def flat(mine):
            return mine.swapaxes(0, 1).reshape((FB,) + mine.shape[2:])

        a_got = swap(a_other, "seq", 2)
        all_a = flat(fold([a_mine], [a_got], "fold_a_y")[0])
        b_mine = [p[:, 0] for p in (b_mine, b_other)], [p[:, 1] for p in (b_mine, b_other)]
        b_got = [swap(p, "seq", 2) for p in b_mine[1]]
        all_b = flat(jnp.stack(fold(b_mine[0], b_got, "fold_b_y")))
        fc = all_a[:, :ROWS].reshape(FB, ROWS, split, FC // split).transpose(0, 2, 1, 3)
        sum_fc = plain(fc.reshape(dp, ROWS, FC // split))
        go = all_a[:, ROWS:].reshape(FB, HALF, 2, ROWS).transpose(0, 2, 1, 3)
        sum_out = plain(go.reshape(dp, D // dp, ROWS)).T
        proj = all_b.reshape(FB, 2, DB, FC).transpose(0, 2, 1, 3)
        sum_proj = plain(proj.reshape(dp, D // dp, D)).T
        all_q = flat(jnp.stack([q_keep, q_send]))
        halves = [all_q[:, :QH, :ROWS], all_q[:, :QH, ROWS:]]
        sum_qkv = plain(jnp.concatenate(halves, 1).reshape(dp, 3 * D // dp, ROWS)).T
        vrows = all_q[:, QH].reshape(FB, 4, DB)[:, :3]
        vrows = vrows.reshape(FB, 3, split, DB // split).transpose(0, 2, 1, 3)
        sum_vec = plain(vrows.reshape(dp, 3, DB // split))
    (input_grad,) = call(
        last_kernel, [dx1, own, other, x[0], vec], [shape((TOK, D), bf16)], [], 0.3, "last"
    )

    qkv_set = (qkv_weight, qkv_first, qkv_second)
    out_set = (out_weight, out_first, out_second)
    fc_set = (fc_weight, fc_first, fc_second)
    proj_set = (proj_weight, proj_first, proj_second)
    vec_set = (vectors, vector_first, vector_second)
    if by_pairs:

        def news(group):
            return [shape(group[0].shape, d) for d in (f32, f32, f32, bf16)]

        def turned(group):
            return [v.T for v in group]

        proj_set = turned(proj_set)

        proj_new = call(
            adam_b_kernel, [proj, proj_got, *proj_set], news(proj_set), [], 0.3, "adam_proj"
        )
        proj_new = turned(proj_new)
        new = call(
            adam_a_kernel, [*a_pieces, *fc_set, *out_set], news(fc_set) + news(out_set),
            [], 0.3, "adam_fc", deps=[input_grad, proj_new[0].T],
        )
        fc_new, out_new = new[:4], new[4:]
        new = call(
            adam_q_kernel, [*q_pieces, *qkv_set, *vec_set], news(qkv_set) + news(vec_set),
            [], 0.3, "adam_qkv", deps=[fc_new[0]],
        )
        qkv_new, vec_new = new[:4], new[4:]
    else:
        qkv_new = adam_update(*qkv_set, sum_qkv, D ** (-0.5), matrix_decay)
        out_new = adam_update(*out_set, sum_out, max(1, 16 * D // LEN) ** (-0.5), matrix_decay)
        fc_new = adam_update(*fc_set, sum_fc, D ** (-0.5), matrix_decay)
        proj_new = adam_update(*proj_set, sum_proj, FF ** (-0.5), matrix_decay)
        vec_new = adam_update(*vec_set, sum_vec, 0.5, 0.0)
    return (
        out.reshape(inputs.shape),
        input_grad.reshape(inputs.shape),
        *qkv_new,
        *out_new,
        *fc_new,
        *proj_new,
        *vec_new,
    )


def solution(mesh):
    rows = P("dp", "seq", None)
    block = P("seq", "dp")
    return jax.shard_map(
        local,
        mesh=mesh,
        in_specs=(rows, rows) + (block,) * 15,
        out_specs=(rows, rows) + (block,) * 20,
        check_vma=False,
    )
```
